256 devices in a mesh: row: 16 (over z, y_hi), col: 16 (over y_lo, x, core).
Axes of the slice: x: 4, y: 4 (y_hi: 2, y_lo: 2; y = y_hi * 2 + y_lo), z: 8, core: 2. Of those that a mesh axis runs over, the one named last changes fastest.
Arguments:
- anc_inverse: float32 [20480, 20480], P('row', 'col'), may hold values from -6 to 6
- l_store: float32 [16, 20480, 256], P('col', 'row'), may hold values from -0.0546875 to 0.0546875
- diag_inv: float32 [16, 256, 256], P('col'), may hold values from -6 to 6
- block_lists: int32 [4, 96], replicated, may hold values from 0 to 159, as said below
- block_counts: int32 [4], replicated, may hold values from 48 to 96, as said below
- sibling_columns: int32 [4], replicated, may hold values from 0 to 15, as said below
Outputs:
- upper_out: float32 [4, 256, 20480], P(None, 'row', 'col')
- lower_out: float32 [16, 20480, 256], P('col', 'row')
- diag_out: float32 [16, 256, 256], P('col')
The draws below stay inside these ranges and needn't reach their ends.
Inputs may be any that keep to these rules, and one draw needn't show every extreme that they name: `block_lists`: in each sibling's row the entries are distinct block indices; entries at positions from block_counts onward are ignored. `block_counts`: some sibling uses all 96 entries. `sibling_columns`: distinct columns for distinct siblings.
All inputs are finite; a program needn't handle non-finite values.
Results may differ from the reference program's by a relative error of at most 0.00011.
Values sent between devices are 32-bit elements; how exact they have to be, the bound alone decides.
No kernel may reach another device: no remote copies, remote signals or barrier semaphores. Data moves between devices by JAX's collectives and lax.ppermute only.
A program may use at most 64 MiB of HBM per device.

```python
import jax
import jax.numpy as jnp
from jax import lax

BLK = 128
NBLK = 160
W = 256
SIB = 4
KMAX = 96
S = 20480
N_COL = 16


def draw_block_lists(key, part):
    sib_keys = jax.random.split(jax.random.fold_in(key, 3), SIB)
    picked = jax.vmap(lambda one_key: jax.random.permutation(one_key, NBLK)[:KMAX])(sib_keys)
    return picked.astype(jnp.int32)


def draw_block_counts(key, part):
    counts = jax.random.randint(jax.random.fold_in(key, 7), (SIB,), KMAX // 2, KMAX + 1)
    pick_one = jax.random.randint(jax.random.fold_in(key, 8), (), 0, SIB)
    counts = jnp.where(jnp.arange(SIB) == pick_one, KMAX, counts)
    return counts.astype(jnp.int32)


def draw_sibling_columns(key, part):
    column_order = jax.random.permutation(jax.random.fold_in(key, 11), N_COL)
    return column_order[:SIB].astype(jnp.int32)


def block_levels(key, dims, cuts, smallest, high):
    def one(axis_at, parts):
        draws = jax.random.uniform(jax.random.fold_in(jax.random.fold_in(key, 6), axis_at), (parts,), jnp.float32, smallest / len(cuts), high / len(cuts))
        return jnp.repeat(jnp.exp(draws), dims[axis_at] // parts).reshape((-1,) + (1,) * (len(dims) - axis_at - 1))

    level = one(*cuts[0])
    for cut in cuts[1:]:
        level = level * one(*cut)
    return level


def gaussian(own_key, extent, scale, limit, cuts=(), kind=jnp.bfloat16):
    result = scale * jax.random.normal(own_key, extent, jnp.float32)
    if cuts:
        result = result * block_levels(own_key, extent, cuts, -0.22, 0.18)
    return jnp.clip(result, -limit, limit).astype(kind)


def setup_inputs(seed: int = 0) -> dict:
    streams_of = jax.random.split(jax.random.key(seed), 7)
    anc_inverse = gaussian(streams_of[0], (S, S), 1.0, 6.0, ((0, 16), (1, 16)), jnp.float32)
    l_store = gaussian(streams_of[1], (N_COL, S, W), (KMAX * BLK) ** -0.5, 0.0546875, ((0, 16), (1, 16)), jnp.float32)
    diag_inv = gaussian(streams_of[2], (N_COL, W, W), 1.0, 6.0, ((0, 16),), jnp.float32)
    block_lists = draw_block_lists(jax.random.fold_in(streams_of[6], 71), 0)
    block_counts = draw_block_counts(jax.random.fold_in(streams_of[6], 71), 0)
    sibling_columns = draw_sibling_columns(jax.random.fold_in(streams_of[6], 71), 0)
    return dict(anc_inverse=anc_inverse, l_store=l_store, diag_inv=diag_inv, block_lists=block_lists, block_counts=block_counts, sibling_columns=sibling_columns)


def member_mask(block_lists, block_counts):
    block_ids = jnp.arange(NBLK, dtype=jnp.int32)
    valid_entry = jnp.arange(KMAX, dtype=jnp.int32)[None, :] < block_counts[:, None]
    entry_hits = (block_lists[:, :, None] == block_ids[None, None, :]) & valid_entry[:, :, None]
    return jnp.repeat(jnp.any(entry_hits, axis=1).astype(jnp.float32), BLK, axis=1)


def reference(anc_inverse, l_store, diag_inv, block_lists, block_counts, sibling_columns):
    listed = member_mask(block_lists, block_counts)
    panels = l_store[sibling_columns.astype(jnp.int32)] * listed[:, :, None]
    upper_out = -jnp.einsum("jsw,st->jwt", panels, anc_inverse, precision=lax.Precision.HIGHEST, preferred_element_type=jnp.float32) * listed[:, None, :]
    inner_sum = jnp.einsum("jws,jsv->jwv", upper_out, panels, precision=lax.Precision.HIGHEST, preferred_element_type=jnp.float32)
    chosen = (sibling_columns[:, None] == jnp.arange(N_COL, dtype=jnp.int32)[None, :]).astype(jnp.float32)
    present = jnp.sum(chosen, axis=0)
    lower_out = jnp.einsum("jc,jws->csw", chosen, upper_out, precision=lax.Precision.HIGHEST, preferred_element_type=jnp.float32)
    diag_out = present[:, None, None] * diag_inv - jnp.einsum("jc,jwv->cwv", chosen, inner_sum, precision=lax.Precision.HIGHEST, preferred_element_type=jnp.float32)
    return upper_out, lower_out, diag_out
```

```python
import jax
import jax.numpy as jnp
from jax import lax
from jax.sharding import Mesh
from jax.sharding import PartitionSpec as P

BLK = 128
ROW = ("row_0", "row_1")


def listed_blocks(block_lists, block_counts, first_block, block_total):
    block_ids = first_block + jnp.arange(block_total, dtype=jnp.int32)
    valid_entry = jnp.arange(block_lists.shape[1], dtype=jnp.int32)[None, :] < block_counts[:, None]
    entry_hits = (block_lists[:, :, None] == block_ids[None, None, :]) & valid_entry[:, :, None]
    return jnp.repeat(jnp.any(entry_hits, axis=1).astype(jnp.float32), BLK, axis=1)


def summed_over(x, axis):
    parts = lax.all_to_all(x, axis, 0, 0, tiled=True)
    return jnp.sum(parts, axis=0)


def per_device(anc_inverse, l_store, diag_inv, block_lists, block_counts, sibling_columns):
    row_cells, col_cells = anc_inverse.shape
    width = l_store.shape[2]
    sib = sibling_columns.shape[0]
    n_col = lax.axis_size("col")
    n_row = lax.axis_size(ROW)
    row_index = lax.axis_index(ROW)
    col_index = lax.axis_index("col")
    row_mask = listed_blocks(
        block_lists, block_counts, row_index * (row_cells // BLK), row_cells // BLK
    )
    col_mask = listed_blocks(
        block_lists, block_counts, col_index * (col_cells // BLK), col_cells // BLK
    )
    own_slot = l_store[0]
    piece = row_cells // n_col
    scattered = lax.all_to_all(
        own_slot.reshape(n_col, piece, width), "col", 0, 0, tiled=True
    )
    owned = jnp.concatenate(
        [lax.dynamic_index_in_dim(scattered, sibling_columns[j], 0) for j in range(sib)]
    )
    panels = lax.all_gather(owned, "col", axis=0, tiled=False)
    masked = panels * row_mask.reshape(sib, n_col, piece).transpose(1, 0, 2)[..., None]
    partial_value = (
        -jnp.einsum(
            "pjrw,prc->jwc",
            masked,
            anc_inverse.reshape(n_col, piece, col_cells),
            precision=lax.Precision.HIGH,
            preferred_element_type=jnp.float32,
        )
        * col_mask[:, None, :]
    )
    nearer = lax.psum_scatter(partial_value, "row_0", scatter_dimension=1, tiled=True)
    upper_part = lax.psum_scatter(nearer, "row_1", scatter_dimension=1, tiled=True)
    slab = width // n_row
    swap = [
        (r * n_col + c, c * n_col + (r + c) % n_row) for r in range(n_row) for c in range(n_col)
    ]
    moved = lax.ppermute(upper_part, ROW + ("col",), swap)
    slots = jnp.zeros((n_col, slab, col_cells), jnp.float32)
    for j in range(sib):
        slots = lax.dynamic_update_slice_in_dim(slots, moved[j][None], sibling_columns[j], 0)
    gathered = lax.all_to_all(slots, "col", 0, 0, tiled=True)
    ordered = jnp.roll(gathered, -row_index, axis=0)
    picked = ordered.reshape(width, col_cells)
    chosen = (sibling_columns == col_index).astype(jnp.float32)
    own_mask = jnp.sum(chosen[:, None] * row_mask, axis=0)
    own_panel = own_slot * own_mask[:, None]
    inner_part = jnp.dot(
        picked, own_panel, precision=lax.Precision.HIGH, preferred_element_type=jnp.float32
    )
    own_rows = summed_over(inner_part.reshape(n_row, width // n_row, width), ROW)
    total = lax.all_to_all(
        jnp.broadcast_to(own_rows[None], (n_row, *own_rows.shape)), ROW, 0, 0, tiled=True
    )
    diag_total = total.reshape(width, width)
    present = jnp.sum(chosen)
    diag_out = (present * diag_inv[0] - diag_total)[None]
    lower_out = jnp.transpose(picked)[None]
    return (upper_part, lower_out, diag_out)


def solution(mesh):
    finer = Mesh(mesh.devices.reshape(8, 2, mesh.shape["col"]), ("row_0", "row_1", "col"))
    return jax.shard_map(
        per_device,
        mesh=finer,
        in_specs=(P(ROW, "col"), P("col", ROW, None), P("col", None, None), P(), P(), P()),
        out_specs=(P(None, ROW, "col"), P("col", ROW, None), P("col", None, None)),
        check_vma=False,
    )
```

```python
import jax
import jax.numpy as jnp
from jax import lax
from jax.sharding import Mesh
from jax.sharding import PartitionSpec as P

BLK = 128
ROW = ("row_0", "row_1")


def listed_blocks(block_lists, block_counts, first_block, block_total):
    block_ids = first_block + jnp.arange(block_total, dtype=jnp.int32)
    valid_entry = jnp.arange(block_lists.shape[1], dtype=jnp.int32)[None, :] < block_counts[:, None]
    entry_hits = (block_lists[:, :, None] == block_ids[None, None, :]) & valid_entry[:, :, None]
    return jnp.repeat(jnp.any(entry_hits, axis=1).astype(jnp.float32), BLK, axis=1)


def swapped(x, axis, bit):
    length = lax.axis_size(axis)
    return lax.ppermute(x, axis, [(i, i ^ bit) for i in range(length)])


def per_device(anc_inverse, l_store, diag_inv, block_lists, block_counts, sibling_columns):
    row_cells, col_cells = anc_inverse.shape
    width = l_store.shape[2]
    sib = sibling_columns.shape[0]
    n_col = lax.axis_size("col")
    n_row = lax.axis_size(ROW)
    row_index = lax.axis_index(ROW)
    col_index = lax.axis_index("col")
    row_mask = listed_blocks(
        block_lists, block_counts, row_index * (row_cells // BLK), row_cells // BLK
    )
    col_mask = listed_blocks(
        block_lists, block_counts, col_index * (col_cells // BLK), col_cells // BLK
    )
    own_slot = l_store[0]
    piece = row_cells // n_col
    scattered = lax.all_to_all(
        own_slot.reshape(n_col, piece, width), "col", 0, 0, tiled=True
    )
    owned = jnp.concatenate(
        [lax.dynamic_index_in_dim(scattered, sibling_columns[j], 0) for j in range(sib)]
    )
    panels = lax.all_gather(owned, "col", axis=0, tiled=False)
    masked = panels * row_mask.reshape(sib, n_col, piece).transpose(1, 0, 2)[..., None]
    partial_value = (
        -jnp.einsum(
            "pjrw,prc->jwc",
            masked,
            anc_inverse.reshape(n_col, piece, col_cells),
            precision=lax.Precision.HIGH,
            preferred_element_type=jnp.float32,
        )
        * col_mask[:, None, :]
    )
    nearer = lax.psum_scatter(partial_value, "row_0", scatter_dimension=1, tiled=True)
    slab = width // n_row
    half = lax.axis_index("row_1")
    sent = lax.dynamic_slice_in_dim(nearer, (1 - half) * slab, slab, 1)
    kept = lax.dynamic_slice_in_dim(nearer, half * slab, slab, 1)
    upper_part = kept + swapped(sent, "row_1", 1)
    by_width = lax.all_to_all(upper_part.transpose(1, 0, 2), "col", 0, 0, tiled=True)
    moved = lax.all_to_all(by_width, ROW, 0, 0, tiled=True)
    slots = jnp.zeros((n_col, n_row, col_cells), jnp.float32)
    for j in range(sib):
        slots = lax.dynamic_update_slice_in_dim(slots, moved[None, :, j], sibling_columns[j], 0)
    gathered = lax.all_to_all(slots, "col", 0, 0, tiled=True)
    whole_panels = masked.transpose(1, 0, 2, 3).reshape(sib, row_cells, width)
    inner = jnp.einsum(
        "rjt,jtv->jrv",
        moved,
        whole_panels,
        precision=lax.Precision.HIGH,
        preferred_element_type=jnp.float32,
    )
    inner = inner + swapped(inner, "row_1", 1)
    for step in (1, 2, 4):
        inner = inner + swapped(inner, "row_0", step)
    gathered, inner = lax.optimization_barrier((gathered, inner))
    diag_slots = jnp.zeros((n_col, n_row, width), jnp.float32)
    for j in range(sib):
        diag_slots = lax.dynamic_update_slice_in_dim(
            diag_slots, inner[j][None], sibling_columns[j], 0
        )
    diag_parts = lax.all_to_all(diag_slots, "col", 0, 0, tiled=True)
    lower_out = gathered.transpose(2, 1, 0).reshape(1, row_cells, width)
    diag_total = diag_parts.transpose(1, 0, 2).reshape(width, width)
    present = jnp.sum((sibling_columns == col_index).astype(jnp.float32))
    diag_out = (present * diag_inv[0] - diag_total)[None]
    return (upper_part, lower_out, diag_out)


def solution(mesh):
    finer = Mesh(mesh.devices.reshape(8, 2, mesh.shape["col"]), ("row_0", "row_1", "col"))
    return jax.shard_map(
        per_device,
        mesh=finer,
        in_specs=(P(ROW, "col"), P("col", ROW, None), P("col", None, None), P(), P(), P()),
        out_specs=(P(None, ROW, "col"), P("col", ROW, None), P("col", None, None)),
        check_vma=False,
    )
```

```python
import functools

import jax
import jax.numpy as jnp
from jax import lax
from jax.experimental import pallas as pl
from jax.experimental.pallas import tpu as pltpu
from jax.sharding import Mesh
from jax.sharding import PartitionSpec as P

BLK = 128
SUB = 8
ROW = ("row_0", "row_1")
COL = ("col_y", "col_x", "core")
CAPS = (28,)

ROW_BLOCK, ROW_START, COL_BLOCK, COL_START = 0, 64, 72, 136
PIECE, ROW_SLOT, COL_SLOT, SOURCE, HALF, TABLE = 144, 160, 224, 288, 352, 360

SMEM = pl.BlockSpec(memory_space=pltpu.SMEM)
VMEM = pl.BlockSpec(memory_space=pltpu.VMEM)


def swapped(x, axis, bit):
    length = lax.axis_size(axis)
    return lax.ppermute(x, axis, [(i, i ^ bit) for i in range(length)])


def turned(x, axis, shift):
    length = lax.axis_size(axis)
    return lax.ppermute(x, axis, [(i, (i + shift) % length) for i in range(length)])


def member_blocks(block_lists, block_counts, block_total):
    block_ids = jnp.arange(block_total, dtype=jnp.int32)
    valid_entry = jnp.arange(block_lists.shape[1], dtype=jnp.int32)[None, :] < block_counts[:, None]
    entry_hits = (block_lists[:, :, None] == block_ids[None, None, :]) & valid_entry[:, :, None]
    return jnp.any(entry_hits, axis=1).astype(jnp.int32)


def slot_tables(listed):
    sib, blocks = listed.shape
    flat = listed.reshape(-1)
    place = jnp.arange(sib * blocks, dtype=jnp.int32)
    before = jnp.sum(jnp.where(place[None, :] < place[:, None], flat[None, :], 0), axis=1)
    here = (before[None, :] == place[:, None]) & (flat[None, :] > 0)
    code = jnp.sum(jnp.where(here, place[None, :], 0), axis=1)
    bounds = jnp.arange(sib + 1, dtype=jnp.int32) * blocks
    start = jnp.sum(jnp.where(place[None, :] < bounds[:, None], flat[None, :], 0), axis=1)
    slot = jnp.where(flat > 0, before, -1)
    return code, start, slot


def padded(values, length):
    return jnp.pad(values.astype(jnp.int32), (0, length - values.shape[0]))


def pick_kernel(cap, tab, x_ref, o_ref):
    for q in range(cap):
        o_ref[q] = x_ref[tab[SOURCE + q]]


def product_kernel(cap, sib, tab, g0, g1, c0, c1, ah, al, u_ref, p_ref, lhs, acc):
    parts = (g0, g1, c0, c1)
    for i in range(4 * len(parts)):
        at = pl.multiple_of(tab[PIECE + i] * SUB, SUB)
        p_ref[:, pl.ds(at, SUB), :] = parts[i // 4][i % 4]
    chunks, _, rows, _ = u_ref.shape

    def tile(ref, b, t):
        return ref[
            pl.ds(pl.multiple_of(b * BLK, BLK), BLK), pl.ds(pl.multiple_of(t * BLK, BLK), BLK)
        ]

    def square(ref, b0, b1, t0, t1):
        top = jnp.concatenate([tile(ref, b0, t0), tile(ref, b0, t1)], axis=1)
        low = jnp.concatenate([tile(ref, b1, t0), tile(ref, b1, t1)], axis=1)
        return jnp.concatenate([top, low], axis=0)

    for j in range(sib):
        r0 = tab[ROW_START + j]
        r1 = tab[ROW_START + j + 1]
        n0 = tab[COL_START + j]
        n1 = tab[COL_START + j + 1]
        pairs = (r1 - r0 + 1) // 2

        def split(i, carry, r0=r0, r1=r1):
            q = r0 + 2 * i
            second = jnp.where(q + 1 < r1, p_ref[jnp.minimum(q + 1, cap - 1)], 0.0)
            block = jnp.concatenate([p_ref[q], second], axis=0).T
            hi = block.astype(jnp.bfloat16)
            lo = (block - hi.astype(jnp.float32)).astype(jnp.bfloat16)
            lhs[i] = jnp.concatenate([hi, hi, lo], axis=1)
            return carry

        lax.fori_loop(0, pairs, split, 0)

        def columns(o, carry, r0=r0, n0=n0, n1=n1, pairs=pairs):
            s = n0 + 2 * o
            t0 = tab[COL_BLOCK + s]
            t1 = tab[COL_BLOCK + s + 1]
            acc[...] = jnp.zeros_like(acc)

            def rows_of(i, inner):
                b0 = tab[ROW_BLOCK + r0 + 2 * i]
                b1 = tab[ROW_BLOCK + r0 + 2 * i + 1]
                hi = square(ah, b0, b1, t0, t1)
                lo = square(al, b0, b1, t0, t1)
                acc[...] += jnp.dot(
                    lhs[i],
                    jnp.concatenate([hi, lo, hi], axis=0),
                    preferred_element_type=jnp.float32,
                )
                return inner

            lax.fori_loop(0, pairs, rows_of, 0)
            for z in range(chunks):
                u_ref[z, s] = -acc[z * rows : (z + 1) * rows, :BLK]

            @pl.when(s + 1 < n1)
            def _():
                for z in range(chunks):
                    u_ref[z, s + 1] = -acc[z * rows : (z + 1) * rows, BLK:]

            return carry

        lax.fori_loop(0, (n1 - n0 + 1) // 2, columns, 0)

    def clear(s, carry):
        u_ref[:, s] = jnp.zeros((chunks, rows, BLK), jnp.float32)
        return carry

    lax.fori_loop(tab[COL_START + sib], cap, clear, 0)


def spread_kernel(tab, p_ref, o_ref):
    def one(i, carry):
        slot = tab[ROW_SLOT + i]
        o_ref[i] = jnp.where(slot >= 0, p_ref[jnp.maximum(slot, 0)], 0.0)
        return carry

    lax.fori_loop(0, o_ref.shape[0], one, 0)


def unpack_kernel(tab, near_ref, got_ref, o_ref):
    sib, slab, cells = o_ref.shape
    blocks = cells // BLK
    at = pl.multiple_of(tab[HALF] * slab, SUB)
    for j in range(sib):
        for b in range(blocks):
            slot = tab[COL_SLOT + j * blocks + b]
            use = jnp.maximum(slot, 0)
            total = near_ref[use, pl.ds(at, slab), :] + got_ref[use]
            o_ref[j, :, b * BLK : (b + 1) * BLK] = jnp.where(slot >= 0, total, 0.0)


def listed_products(cap, sib, table, scattered, a_hi, a_lo):
    row_cells, col_cells = a_hi.shape
    pieces, blocks, sub, width = scattered.shape
    near_chunks = lax.axis_size("row_0")
    half_rows = width // (near_chunks * lax.axis_size("row_1"))
    own = pl.pallas_call(
        functools.partial(pick_kernel, cap),
        out_shape=jax.ShapeDtypeStruct((cap, sub, width), jnp.float32),
        in_specs=[SMEM, VMEM],
        out_specs=VMEM,
        compiler_params=pltpu.CompilerParams(vmem_limit_bytes=8 << 20),
    )(table, scattered.reshape(pieces * blocks, sub, width))
    right = turned(own, "col_x", 1)
    left = turned(own, "col_x", -1)
    beside = swapped(own, "col_y", 1)
    right_beside = turned(beside, "col_x", 1)
    left_beside = turned(beside, "col_x", -1)
    right_two = turned(right, "col_x", 1)
    left_two = turned(left_beside, "col_x", -1)
    g0 = jnp.stack([own, beside, right, left])
    g1 = jnp.stack([right_beside, left_beside, right_two, left_two])
    c0 = swapped(g0, "core", 1)
    c1 = swapped(g1, "core", 1)
    chunk = width // near_chunks
    u, p = pl.pallas_call(
        functools.partial(product_kernel, cap, sib),
        out_shape=(
            jax.ShapeDtypeStruct((near_chunks, cap, chunk, BLK), jnp.float32),
            jax.ShapeDtypeStruct((cap, BLK, width), jnp.float32),
        ),
        in_specs=[SMEM] + [VMEM] * 6,
        out_specs=(VMEM, VMEM),
        scratch_shapes=[
            pltpu.VMEM((row_cells // BLK // 2, width, 6 * BLK), jnp.bfloat16),
            pltpu.VMEM((width, 2 * BLK), jnp.float32),
        ],
        compiler_params=pltpu.CompilerParams(vmem_limit_bytes=40 << 20),
    )(table, g0, g1, c0, c1, a_hi, a_lo)
    near = lax.psum_scatter(u, "row_0", scatter_dimension=0, tiled=True)[0]
    panels = pl.pallas_call(
        spread_kernel,
        out_shape=jax.ShapeDtypeStruct((sib * row_cells // BLK, BLK, width), jnp.float32),
        in_specs=[SMEM, VMEM],
        out_specs=VMEM,
        compiler_params=pltpu.CompilerParams(vmem_limit_bytes=16 << 20),
        cost_estimate=pl.CostEstimate(flops=0, transcendentals=0, bytes_accessed=10 << 20),
    )(table, p)
    half = lax.axis_index("row_1")
    sent = lax.dynamic_slice_in_dim(near, (1 - half) * half_rows, half_rows, 1)
    got = swapped(sent, "row_1", 1)
    upper_part = pl.pallas_call(
        unpack_kernel,
        out_shape=jax.ShapeDtypeStruct((sib, half_rows, col_cells), jnp.float32),
        in_specs=[SMEM, VMEM, VMEM],
        out_specs=VMEM,
        compiler_params=pltpu.CompilerParams(vmem_limit_bytes=8 << 20),
    )(table, near, got)
    return upper_part, panels


def piece_columns():
    y = lax.axis_index("col_y")
    x = lax.axis_index("col_x")
    core = lax.axis_index("core")
    n_x = lax.axis_size("col_x")
    places = [(y, x), (1 - y, x), (y, x - 1), (y, x + 1)]
    places += [(1 - y, x - 1), (1 - y, x + 1), (y, x - 2), (1 - y, x + 2)]
    return jnp.stack(
        [
            (py * n_x + (px + n_x) % n_x) * 2 + pc
            for pc in (core, 1 - core)
            for py, px in places
        ]
    ).astype(jnp.int32)


def per_device(anc_inverse, l_store, diag_inv, block_lists, block_counts, sibling_columns):
    row_cells, col_cells = anc_inverse.shape
    width = l_store.shape[2]
    sib = sibling_columns.shape[0]
    n_col = lax.axis_size(COL)
    n_row = lax.axis_size(ROW)
    row_index = lax.axis_index(ROW)
    col_index = lax.axis_index(COL)
    blocks = row_cells // BLK
    cut = l_store[0].reshape(blocks, n_col, SUB, width).transpose(1, 0, 2, 3)
    scattered = lax.all_to_all(cut, COL, 0, 0, tiled=True)
    rounded = lax.reduce_precision(anc_inverse, 8, 7)
    a_hi = rounded.astype(jnp.bfloat16)
    a_lo = (anc_inverse - rounded).astype(jnp.bfloat16)

    listed = member_blocks(block_lists, block_counts, n_row * blocks)
    groups = listed.reshape(sib, n_row, blocks)
    most = jnp.max(jnp.sum(groups, axis=(0, 2)))
    row_code, row_start, row_slot = slot_tables(
        lax.dynamic_index_in_dim(groups, row_index, 1, keepdims=False)
    )
    col_code, col_start, col_slot = slot_tables(
        lax.dynamic_index_in_dim(groups, col_index, 1, keepdims=False)
    )
    owner = jnp.sum(
        jnp.where(
            (row_code // blocks)[:, None] == jnp.arange(sib, dtype=jnp.int32)[None, :],
            sibling_columns[None, :],
            0,
        ),
        axis=1,
    )
    table = jnp.concatenate(
        [
            padded(row_code % blocks, 64),
            padded(row_start, 8),
            padded(col_code % blocks, 64),
            padded(col_start, 8),
            padded(piece_columns(), 16),
            padded(row_slot, 64),
            padded(col_slot, 64),
            padded(owner * blocks + row_code % blocks, 64),
            padded(lax.axis_index("row_1")[None], 8),
        ]
    )
    caps = [c for c in CAPS if c < sib * blocks] + [sib * blocks]
    which = sum((most > c).astype(jnp.int32) for c in caps[:-1])
    upper_part, panels = lax.switch(
        which,
        [functools.partial(listed_products, c, sib) for c in caps],
        table,
        scattered,
        a_hi,
        a_lo,
    )
    by_width = lax.all_to_all(upper_part.transpose(1, 0, 2), COL, 0, 0, tiled=True)
    moved = lax.all_to_all(by_width, ROW, 0, 0, tiled=True)
    slots = jnp.zeros((n_col, n_row, col_cells), jnp.float32)
    for j in range(sib):
        slots = lax.dynamic_update_slice_in_dim(slots, moved[None, :, j], sibling_columns[j], 0)
    gathered = lax.all_to_all(slots, COL, 0, 0, tiled=True)
    inner = jnp.einsum(
        "rjt,jtv->jrv",
        moved,
        panels.reshape(sib, row_cells, width),
        precision=lax.Precision.HIGH,
        preferred_element_type=jnp.float32,
    )
    inner = inner + swapped(inner, "row_1", 1)
    for step in (1, 2, 4):
        inner = inner + swapped(inner, "row_0", step)
    gathered, inner = lax.optimization_barrier((gathered, inner))
    diag_slots = jnp.zeros((n_col, n_row, width), jnp.float32)
    for j in range(sib):
        diag_slots = lax.dynamic_update_slice_in_dim(
            diag_slots, inner[j][None], sibling_columns[j], 0
        )
    diag_parts = lax.all_to_all(diag_slots, COL, 0, 0, tiled=True)
    lower_out = gathered.transpose(2, 1, 0).reshape(1, row_cells, width)
    diag_total = diag_parts.transpose(1, 0, 2).reshape(width, width)
    present = jnp.sum((sibling_columns == col_index).astype(jnp.float32))
    diag_out = (present * diag_inv[0] - diag_total)[None]
    return (upper_part, lower_out, diag_out)


def solution(mesh):
    finer = Mesh(mesh.devices.reshape(8, 2, 2, 4, 2), ROW + COL)
    return jax.shard_map(
        per_device,
        mesh=finer,
        in_specs=(P(ROW, COL), P(COL, ROW, None), P(COL, None, None), P(), P(), P()),
        out_specs=(P(None, ROW, COL), P(COL, ROW, None), P(COL, None, None)),
        check_vma=False,
    )
```

```python
import functools

import jax
import jax.numpy as jnp
from jax import lax
from jax.experimental import pallas as pl
from jax.experimental.pallas import tpu as pltpu
from jax.sharding import Mesh
from jax.sharding import PartitionSpec as P

BLK = 128
SUB = 8
ROW = ("row_0", "row_1")
COL = ("col_y", "col_x", "core")
CAPS = (28,)

ROW_BLOCK, ROW_START, COL_BLOCK, COL_START = 0, 64, 72, 136
PIECE, ROW_SLOT, COL_SLOT, SOURCE, OWNER, PRESENT, AT_ROW = 144, 160, 224, 288, 352, 360, 361

SMEM = pl.BlockSpec(memory_space=pltpu.SMEM)
VMEM = pl.BlockSpec(memory_space=pltpu.VMEM)


def swapped(x, axis, bit):
    length = lax.axis_size(axis)
    return lax.ppermute(x, axis, [(i, i ^ bit) for i in range(length)])


def turned(x, axis, shift):
    length = lax.axis_size(axis)
    return lax.ppermute(x, axis, [(i, (i + shift) % length) for i in range(length)])


def member_blocks(block_lists, block_counts, block_total):
    block_ids = jnp.arange(block_total, dtype=jnp.int32)
    valid_entry = jnp.arange(block_lists.shape[1], dtype=jnp.int32)[None, :] < block_counts[:, None]
    entry_hits = (block_lists[:, :, None] == block_ids[None, None, :]) & valid_entry[:, :, None]
    return jnp.any(entry_hits, axis=1).astype(jnp.int32)


def slot_tables(listed):
    sib, blocks = listed.shape
    flat = listed.reshape(-1)
    place = jnp.arange(sib * blocks, dtype=jnp.int32)
    before = jnp.sum(jnp.where(place[None, :] < place[:, None], flat[None, :], 0), axis=1)
    here = (before[None, :] == place[:, None]) & (flat[None, :] > 0)
    code = jnp.sum(jnp.where(here, place[None, :], 0), axis=1)
    bounds = jnp.arange(sib + 1, dtype=jnp.int32) * blocks
    start = jnp.sum(jnp.where(place[None, :] < bounds[:, None], flat[None, :], 0), axis=1)
    slot = jnp.where(flat > 0, before, -1)
    return code, start, slot


def padded(values, length):
    return jnp.pad(values.astype(jnp.int32), (0, length - values.shape[0]))


def pick_kernel(cap, tab, x_ref, o_ref):
    def one(q, carry):
        o_ref[q] = x_ref[tab[SOURCE + q]]
        return carry

    lax.fori_loop(0, cap, one, 0)


def product_kernel(cap, sib, tab, g0, g1, c0, c1, ah, al, u_ref, p_ref, lhs, acc):
    parts = (g0, g1, c0, c1)
    for i in range(4 * len(parts)):
        at = pl.multiple_of(tab[PIECE + i] * SUB, SUB)
        p_ref[:, pl.ds(at, SUB), :] = parts[i // 4][i % 4]
    chunks, _, rows, _ = u_ref.shape

    def tile(ref, b, t):
        return ref[
            pl.ds(pl.multiple_of(b * BLK, BLK), BLK), pl.ds(pl.multiple_of(t * BLK, BLK), BLK)
        ]

    def square(ref, b0, b1, t0, t1):
        top = jnp.concatenate([tile(ref, b0, t0), tile(ref, b0, t1)], axis=1)
        low = jnp.concatenate([tile(ref, b1, t0), tile(ref, b1, t1)], axis=1)
        return jnp.concatenate([top, low], axis=0)

    def sibling(j, outer):
        r0 = tab[ROW_START + j]
        r1 = tab[ROW_START + j + 1]
        n0 = tab[COL_START + j]
        n1 = tab[COL_START + j + 1]
        pairs = (r1 - r0 + 1) // 2

        def split(i, carry):
            q = r0 + 2 * i
            second = jnp.where(q + 1 < r1, p_ref[jnp.minimum(q + 1, cap - 1)], 0.0)
            block = jnp.concatenate([p_ref[q], second], axis=0).T
            hi = block.astype(jnp.bfloat16)
            lo = (block - hi.astype(jnp.float32)).astype(jnp.bfloat16)
            lhs[i] = jnp.concatenate([hi, hi, lo], axis=1)
            return carry

        lax.fori_loop(0, pairs, split, 0)

        def columns(o, carry):
            s = n0 + 2 * o
            t0 = tab[COL_BLOCK + s]
            t1 = tab[COL_BLOCK + s + 1]
            acc[...] = jnp.zeros_like(acc)

            def rows_of(i, inner):
                b0 = tab[ROW_BLOCK + r0 + 2 * i]
                b1 = tab[ROW_BLOCK + r0 + 2 * i + 1]
                hi = square(ah, b0, b1, t0, t1)
                lo = square(al, b0, b1, t0, t1)
                acc[...] += jnp.dot(
                    lhs[i],
                    jnp.concatenate([hi, lo, hi], axis=0),
                    preferred_element_type=jnp.float32,
                )
                return inner

            lax.fori_loop(0, pairs, rows_of, 0)
            for z in range(chunks):
                u_ref[z, s] = -acc[z * rows : (z + 1) * rows, :BLK]

            @pl.when(s + 1 < n1)
            def _():
                for z in range(chunks):
                    u_ref[z, s + 1] = -acc[z * rows : (z + 1) * rows, BLK:]

            return carry

        lax.fori_loop(0, (n1 - n0 + 1) // 2, columns, 0)
        return outer

    lax.fori_loop(0, sib, sibling, 0)

    def clear(s, carry):
        u_ref[:, s] = jnp.zeros((chunks, rows, BLK), jnp.float32)
        return carry

    lax.fori_loop(tab[COL_START + sib], cap, clear, 0)


def unpack_kernel(base, tab, x_ref, o_ref):
    sib, _, cells = o_ref.shape
    blocks = cells // BLK

    def sibling(j, carry):
        for b in range(blocks):
            slot = tab[base + j * blocks + b]
            o_ref[j, :, b * BLK : (b + 1) * BLK] = jnp.where(
                slot >= 0, x_ref[jnp.maximum(slot, 0)], 0.0
            )
        return carry

    lax.fori_loop(0, sib, sibling, 0)


def inner_kernel(sib, tab, x_ref, hi_ref, lo_ref, o_ref):
    def sibling(j, carry):
        def one(q, total):
            x = x_ref[q]
            x_hi = x.astype(jnp.bfloat16)
            x_lo = (x - x_hi.astype(jnp.float32)).astype(jnp.bfloat16)
            hi = hi_ref[q]
            return total + jnp.dot(
                jnp.concatenate([x_hi, x_lo, x_hi], axis=1),
                jnp.concatenate([hi, hi, lo_ref[q]], axis=0),
                preferred_element_type=jnp.float32,
            )

        o_ref[j] = lax.fori_loop(
            tab[ROW_START + j],
            tab[ROW_START + j + 1],
            one,
            jnp.zeros(o_ref.shape[1:], jnp.float32),
        )
        return carry

    lax.fori_loop(0, sib, sibling, 0)


def slots_kernel(tab, x_ref, inner_ref, o_ref):
    sib, _, cells = x_ref.shape

    def clear(d, carry):
        o_ref[d] = jnp.zeros(o_ref.shape[1:], jnp.float32)
        return carry

    lax.fori_loop(0, o_ref.shape[0], clear, 0)
    for j in range(sib):
        at = tab[OWNER + j]
        o_ref[at, :, :cells] = x_ref[j]
        o_ref[at, :, cells:] = inner_ref[j]


def finish_kernel(tab, x_ref, diag_ref, lower_ref, out_ref):
    n_row = x_ref.shape[0]
    cells = lower_ref.shape[0]
    places = [lax.rem(2 * n_row - r - tab[AT_ROW], n_row) for r in range(n_row)]
    for b in range(cells // BLK):
        stack = jnp.concatenate([x_ref[p, :, b * BLK : (b + 1) * BLK] for p in places], axis=0)
        lower_ref[b * BLK : (b + 1) * BLK, :] = stack.T
    total = jnp.concatenate([x_ref[p, :, cells:] for p in places], axis=0)
    out_ref[...] = jnp.where(tab[PRESENT] > 0, diag_ref[...] - total, 0.0)


def ring_term(u, z, first, last):
    part = lax.dynamic_index_in_dim(u, (z + 2 * u.shape[0]) % u.shape[0], 0, keepdims=False)
    return part[first:last]


def halves(up, down, half, rows):
    return jnp.concatenate(
        [lax.dynamic_slice_in_dim(x, half * rows, rows, 1) for x in (up, down)]
    )


def listed_products(cap, sib, table, scattered, a_hi, a_lo):
    row_cells, col_cells = a_hi.shape
    pieces, blocks, sub, width = scattered.shape
    near_chunks = lax.axis_size("row_0")
    half_rows = width // (near_chunks * lax.axis_size("row_1"))
    own = pl.pallas_call(
        functools.partial(pick_kernel, cap),
        out_shape=jax.ShapeDtypeStruct((cap, sub, width), jnp.float32),
        in_specs=[SMEM, VMEM],
        out_specs=VMEM,
        compiler_params=pltpu.CompilerParams(vmem_limit_bytes=8 << 20),
    )(table, scattered.reshape(pieces * blocks, sub, width))
    if cap < sib * blocks:
        right = turned(own, "col_x", 1)
        left = turned(own, "col_x", -1)
        beside = swapped(own, "col_y", 1)
        right_beside = turned(beside, "col_x", 1)
        left_beside = turned(beside, "col_x", -1)
        right_two = turned(right, "col_x", 1)
        left_two = turned(left_beside, "col_x", -1)
        g0 = jnp.stack([own, beside, right, left])
        g1 = jnp.stack([right_beside, left_beside, right_two, left_two])
        c0 = swapped(g0, "core", 1)
        c1 = swapped(g1, "core", 1)
    else:
        all_pieces = lax.all_to_all(
            jnp.broadcast_to(own[None], (pieces, *own.shape)), COL, 0, 0, tiled=True
        )
        order = piece_columns()
        parts = jnp.concatenate(
            [lax.dynamic_index_in_dim(all_pieces, order[i], 0) for i in range(pieces)]
        )
        g0, g1, c0, c1 = (parts[i : i + 4] for i in range(0, pieces, 4))
    chunk = width // near_chunks
    u, p = pl.pallas_call(
        functools.partial(product_kernel, cap, sib),
        out_shape=(
            jax.ShapeDtypeStruct((near_chunks, cap, chunk, BLK), jnp.float32),
            jax.ShapeDtypeStruct((cap, BLK, width), jnp.float32),
        ),
        in_specs=[SMEM] + [VMEM] * 6,
        out_specs=(VMEM, VMEM),
        scratch_shapes=[
            pltpu.VMEM((row_cells // BLK // 2, width, 6 * BLK), jnp.bfloat16),
            pltpu.VMEM((width, 2 * BLK), jnp.float32),
        ],
        compiler_params=pltpu.CompilerParams(vmem_limit_bytes=40 << 20),
    )(table, g0, g1, c0, c1, a_hi, a_lo)
    z = lax.axis_index("row_0")
    top = cap // 2
    if cap < sib * blocks:
        up = ring_term(u, z - 1, 0, top)
        down = ring_term(u, z + 1, top, cap)
        for step in range(1, near_chunks):
            up = turned(up, "row_0", 1) + ring_term(u, z - 1 - step, 0, top)
            down = turned(down, "row_0", -1) + ring_term(u, z + 1 + step, top, cap)
    else:
        near = jnp.sum(lax.all_to_all(u, "row_0", 0, 0, tiled=True), axis=0)
        up, down = near[:top], near[top:]
    half = lax.axis_index("row_1")
    sent = halves(up, down, 1 - half, half_rows)
    total = halves(up, down, half, half_rows) + swapped(sent, "row_1", 1)
    unpack = lambda base, x: pl.pallas_call(
        functools.partial(unpack_kernel, base),
        out_shape=jax.ShapeDtypeStruct((sib, half_rows, col_cells), jnp.float32),
        in_specs=[SMEM, VMEM],
        out_specs=VMEM,
        compiler_params=pltpu.CompilerParams(vmem_limit_bytes=8 << 20),
        cost_estimate=pl.CostEstimate(flops=0, transcendentals=0, bytes_accessed=1 << 20),
    )(table, x)
    upper_part = unpack(COL_SLOT, total)
    n_row = lax.axis_size(ROW)
    n_col = lax.axis_size(COL)
    spots = [(r, c) for r in range(n_row) for c in range(n_col)]
    across = [(r * n_col + c, r * n_col + (-r - c) % n_col) for r, c in spots]
    along = [(r * n_col + k, (-r - k) % n_row * n_col + k) for r, k in spots]
    moved = lax.ppermute(lax.ppermute(total, ROW + COL, across), ROW + COL, along)
    p_hi = lax.reduce_precision(p, 8, 7)
    p_lo = (p - p_hi).astype(jnp.bfloat16)
    inner = pl.pallas_call(
        functools.partial(inner_kernel, sib),
        out_shape=jax.ShapeDtypeStruct((sib, half_rows, width), jnp.float32),
        in_specs=[SMEM] + [VMEM] * 3,
        out_specs=VMEM,
        compiler_params=pltpu.CompilerParams(vmem_limit_bytes=12 << 20),
    )(table, moved, p_hi.astype(jnp.bfloat16), p_lo)
    return upper_part, unpack(ROW_SLOT, moved), inner


def piece_columns():
    y = lax.axis_index("col_y")
    x = lax.axis_index("col_x")
    core = lax.axis_index("core")
    n_x = lax.axis_size("col_x")
    places = [(y, x), (1 - y, x), (y, x - 1), (y, x + 1)]
    places += [(1 - y, x - 1), (1 - y, x + 1), (y, x - 2), (1 - y, x + 2)]
    return jnp.stack(
        [
            (py * n_x + (px + n_x) % n_x) * 2 + pc
            for pc in (core, 1 - core)
            for py, px in places
        ]
    ).astype(jnp.int32)


def per_device(anc_inverse, l_store, diag_inv, block_lists, block_counts, sibling_columns):
    row_cells, col_cells = anc_inverse.shape
    width = l_store.shape[2]
    sib = sibling_columns.shape[0]
    n_col = lax.axis_size(COL)
    n_row = lax.axis_size(ROW)
    row_index = lax.axis_index(ROW)
    col_index = lax.axis_index(COL)
    blocks = row_cells // BLK
    cut = l_store[0].reshape(blocks, n_col, SUB, width).transpose(1, 0, 2, 3)
    scattered = lax.all_to_all(cut, COL, 0, 0, tiled=True)
    rounded = lax.reduce_precision(anc_inverse, 8, 7)
    a_hi = rounded.astype(jnp.bfloat16)
    a_lo = (anc_inverse - rounded).astype(jnp.bfloat16)

    listed = member_blocks(block_lists, block_counts, n_row * blocks)
    groups = listed.reshape(sib, n_row, blocks)
    most = jnp.max(jnp.sum(groups, axis=(0, 2)))
    row_code, row_start, row_slot = slot_tables(
        lax.dynamic_index_in_dim(groups, row_index, 1, keepdims=False)
    )
    col_code, col_start, col_slot = slot_tables(
        lax.dynamic_index_in_dim(groups, col_index, 1, keepdims=False)
    )
    owner = jnp.sum(
        jnp.where(
            (row_code // blocks)[:, None] == jnp.arange(sib, dtype=jnp.int32)[None, :],
            sibling_columns[None, :],
            0,
        ),
        axis=1,
    )
    table = jnp.concatenate(
        [
            padded(row_code % blocks, 64),
            padded(row_start, 8),
            padded(col_code % blocks, 64),
            padded(col_start, 8),
            padded(piece_columns(), 16),
            padded(row_slot, 64),
            padded(col_slot, 64),
            padded(owner * blocks + row_code % blocks, 64),
            padded(sibling_columns, 8),
            jnp.stack([jnp.any(sibling_columns == col_index).astype(jnp.int32), row_index]),
        ]
    )
    caps = [c for c in CAPS if c < sib * blocks] + [sib * blocks]
    which = sum((most > c).astype(jnp.int32) for c in caps[:-1])
    upper_part, moved, inner = lax.switch(
        which,
        [functools.partial(listed_products, c, sib) for c in caps],
        table,
        scattered,
        a_hi,
        a_lo,
    )
    bit = 1
    while bit < n_row:
        pairs = [
            (r * n_col + k, (r ^ bit) * n_col + (k + r - (r ^ bit)) % n_col)
            for r in range(n_row)
            for k in range(n_col)
        ]
        inner = inner + lax.ppermute(inner, ROW + COL, pairs)
        bit *= 2
    slots = pl.pallas_call(
        slots_kernel,
        out_shape=jax.ShapeDtypeStruct((n_col, width // n_row, row_cells + width), jnp.float32),
        in_specs=[SMEM] + [VMEM] * 2,
        out_specs=VMEM,
        compiler_params=pltpu.CompilerParams(vmem_limit_bytes=8 << 20),
    )(table, moved, inner)
    gathered = lax.all_to_all(slots, COL, 0, 0, tiled=True)
    lower, diag = pl.pallas_call(
        finish_kernel,
        out_shape=(
            jax.ShapeDtypeStruct((row_cells, width), jnp.float32),
            jax.ShapeDtypeStruct((width, width), jnp.float32),
        ),
        in_specs=[SMEM] + [VMEM] * 2,
        out_specs=(VMEM, VMEM),
        compiler_params=pltpu.CompilerParams(vmem_limit_bytes=12 << 20),
    )(table, gathered, diag_inv[0])
    return (upper_part, lower[None], diag[None])


def solution(mesh):
    finer = Mesh(mesh.devices.reshape(8, 2, 2, 4, 2), ROW + COL)
    return jax.shard_map(
        per_device,
        mesh=finer,
        in_specs=(P(ROW, COL), P(COL, ROW, None), P(COL, None, None), P(), P(), P()),
        out_specs=(P(None, ROW, COL), P(COL, ROW, None), P(COL, None, None)),
        check_vma=False,
    )
```

```python
import functools

import jax
import jax.numpy as jnp
from jax import lax
from jax.experimental import pallas as pl
from jax.experimental.pallas import tpu as pltpu
from jax.sharding import Mesh
from jax.sharding import PartitionSpec as P

BLK = 128
SUB = 8
ROW = ("row_0", "row_1")
COL = ("col_y", "col_x", "core")
CAPS = (28,)

ROW_BLOCK, ROW_START, COL_BLOCK, COL_START = 0, 64, 72, 136
PIECE, ROW_SLOT, COL_SLOT, SOURCE, OWNER, PRESENT, AT_ROW = 144, 160, 224, 288, 352, 360, 361

SMEM = pl.BlockSpec(memory_space=pltpu.SMEM)
VMEM = pl.BlockSpec(memory_space=pltpu.VMEM)


def swapped(x, axis, bit):
    length = lax.axis_size(axis)
    return lax.ppermute(x, axis, [(i, i ^ bit) for i in range(length)])


def turned(x, axis, shift):
    length = lax.axis_size(axis)
    return lax.ppermute(x, axis, [(i, (i + shift) % length) for i in range(length)])


def member_blocks(block_lists, block_counts, block_total):
    block_ids = jnp.arange(block_total, dtype=jnp.int32)
    valid_entry = jnp.arange(block_lists.shape[1], dtype=jnp.int32)[None, :] < block_counts[:, None]
    entry_hits = (block_lists[:, :, None] == block_ids[None, None, :]) & valid_entry[:, :, None]
    return jnp.any(entry_hits, axis=1).astype(jnp.int32)


def slot_tables(listed):
    sib, blocks = listed.shape
    flat = listed.reshape(-1)
    place = jnp.arange(sib * blocks, dtype=jnp.int32)
    before = jnp.sum(jnp.where(place[None, :] < place[:, None], flat[None, :], 0), axis=1)
    here = (before[None, :] == place[:, None]) & (flat[None, :] > 0)
    code = jnp.sum(jnp.where(here, place[None, :], 0), axis=1)
    bounds = jnp.arange(sib + 1, dtype=jnp.int32) * blocks
    start = jnp.sum(jnp.where(place[None, :] < bounds[:, None], flat[None, :], 0), axis=1)
    slot = jnp.where(flat > 0, before, -1)
    return code, start, slot


def padded(values, length):
    return jnp.pad(values.astype(jnp.int32), (0, length - values.shape[0]))


def pick_kernel(cap, tab, x_ref, o_ref):
    def one(q, carry):
        o_ref[q] = x_ref[tab[SOURCE + q]]
        return carry

    lax.fori_loop(0, cap, one, 0)


def product_kernel(cap, sib, tab, g0, g1, c0, c1, ah, al, u_ref, ph_ref, pl_ref, p_ref, lhs, acc):
    parts = (g0, g1, c0, c1)
    for i in range(4 * len(parts)):
        at = pl.multiple_of(tab[PIECE + i] * SUB, SUB)
        p_ref[:, pl.ds(at, SUB), :] = parts[i // 4][i % 4]
    chunks, _, rows, _ = u_ref.shape

    def tile(ref, b, t):
        return ref[
            pl.ds(pl.multiple_of(b * BLK, BLK), BLK), pl.ds(pl.multiple_of(t * BLK, BLK), BLK)
        ]

    def square(ref, b0, b1, t0, t1):
        top = jnp.concatenate([tile(ref, b0, t0), tile(ref, b0, t1)], axis=1)
        low = jnp.concatenate([tile(ref, b1, t0), tile(ref, b1, t1)], axis=1)
        return jnp.concatenate([top, low], axis=0)

    def sibling(j, outer):
        r0 = tab[ROW_START + j]
        r1 = tab[ROW_START + j + 1]
        n0 = tab[COL_START + j]
        n1 = tab[COL_START + j + 1]
        pairs = (r1 - r0 + 1) // 2

        def split(i, carry):
            q = r0 + 2 * i
            second = jnp.where(q + 1 < r1, p_ref[jnp.minimum(q + 1, cap - 1)], 0.0)
            block = jnp.concatenate([p_ref[q], second], axis=0)
            hi = block.astype(jnp.bfloat16)
            lo = (block - hi.astype(jnp.float32)).astype(jnp.bfloat16)
            ph_ref[q] = hi[:BLK]
            pl_ref[q] = lo[:BLK]

            @pl.when(q + 1 < r1)
            def _():
                ph_ref[q + 1] = hi[BLK:]
                pl_ref[q + 1] = lo[BLK:]

            across = hi.T
            lhs[i] = jnp.concatenate([across, across, lo.T], axis=1)
            return carry

        lax.fori_loop(0, pairs, split, 0)

        def columns(o, carry):
            s = n0 + 2 * o
            t0 = tab[COL_BLOCK + s]
            t1 = tab[COL_BLOCK + s + 1]
            acc[...] = jnp.zeros_like(acc)

            def rows_of(i, inner):
                b0 = tab[ROW_BLOCK + r0 + 2 * i]
                b1 = tab[ROW_BLOCK + r0 + 2 * i + 1]
                hi = square(ah, b0, b1, t0, t1)
                lo = square(al, b0, b1, t0, t1)
                acc[...] += jnp.dot(
                    lhs[i],
                    jnp.concatenate([hi, lo, hi], axis=0),
                    preferred_element_type=jnp.float32,
                )
                return inner

            lax.fori_loop(0, pairs, rows_of, 0)
            for z in range(chunks):
                u_ref[z, s] = -acc[z * rows : (z + 1) * rows, :BLK]

            @pl.when(s + 1 < n1)
            def _():
                for z in range(chunks):
                    u_ref[z, s + 1] = -acc[z * rows : (z + 1) * rows, BLK:]

            return carry

        lax.fori_loop(0, (n1 - n0 + 1) // 2, columns, 0)
        return outer

    if cap < sib * (ah.shape[0] // BLK):
        for j in range(sib):
            sibling(j, 0)
    else:
        lax.fori_loop(0, sib, sibling, 0)

    def clear(s, carry):
        u_ref[:, s] = jnp.zeros((chunks, rows, BLK), jnp.float32)
        return carry

    lax.fori_loop(tab[COL_START + sib], cap, clear, 0)


def unpack_kernel(base, tab, x_ref, o_ref):
    sib, _, cells = o_ref.shape
    blocks = cells // BLK

    def sibling(j, carry):
        for b in range(blocks):
            slot = tab[base + j * blocks + b]
            o_ref[j, :, b * BLK : (b + 1) * BLK] = jnp.where(
                slot >= 0, x_ref[jnp.maximum(slot, 0)], 0.0
            )
        return carry

    lax.fori_loop(0, sib, sibling, 0)


def inner_kernel(sib, tab, x_ref, hi_ref, lo_ref, o_ref):
    def sibling(j, carry):
        def one(q, total):
            x = x_ref[q]
            x_hi = x.astype(jnp.bfloat16)
            x_lo = (x - x_hi.astype(jnp.float32)).astype(jnp.bfloat16)
            hi = hi_ref[q]
            return total + jnp.dot(
                jnp.concatenate([x_hi, x_lo, x_hi], axis=1),
                jnp.concatenate([hi, hi, lo_ref[q]], axis=0),
                preferred_element_type=jnp.float32,
            )

        o_ref[j] = lax.fori_loop(
            tab[ROW_START + j],
            tab[ROW_START + j + 1],
            one,
            jnp.zeros(o_ref.shape[1:], jnp.float32),
        )
        return carry

    lax.fori_loop(0, sib, sibling, 0)


def slots_kernel(tab, x_ref, inner_ref, o_ref):
    sib, _, cells = x_ref.shape

    def clear(d, carry):
        o_ref[d] = jnp.zeros(o_ref.shape[1:], jnp.float32)
        return carry

    lax.fori_loop(0, o_ref.shape[0], clear, 0)
    for j in range(sib):
        at = tab[OWNER + j]
        o_ref[at, :, :cells] = x_ref[j]
        o_ref[at, :, cells:] = inner_ref[j]


def finish_kernel(tab, x_ref, diag_ref, lower_ref, out_ref):
    n_row = x_ref.shape[0]
    cells = lower_ref.shape[0]
    places = [lax.rem(2 * n_row - r - tab[AT_ROW], n_row) for r in range(n_row)]
    for b in range(cells // BLK):
        stack = jnp.concatenate([x_ref[p, :, b * BLK : (b + 1) * BLK] for p in places], axis=0)
        lower_ref[b * BLK : (b + 1) * BLK, :] = stack.T
    total = jnp.concatenate([x_ref[p, :, cells:] for p in places], axis=0)
    out_ref[...] = jnp.where(tab[PRESENT] > 0, diag_ref[...] - total, 0.0)


def ring_term(u, z, first, last):
    part = lax.dynamic_index_in_dim(u, (z + 2 * u.shape[0]) % u.shape[0], 0, keepdims=False)
    return part[first:last]


def halves(parts, half, rows):
    return jnp.concatenate([lax.dynamic_slice_in_dim(x, half * rows, rows, 1) for x in parts])


def listed_products(cap, sib, table, scattered, a_hi, a_lo):
    row_cells, col_cells = a_hi.shape
    pieces, blocks, sub, width = scattered.shape
    near_chunks = lax.axis_size("row_0")
    half_rows = width // (near_chunks * lax.axis_size("row_1"))
    own = pl.pallas_call(
        functools.partial(pick_kernel, cap),
        out_shape=jax.ShapeDtypeStruct((cap, sub, width), jnp.float32),
        in_specs=[SMEM, VMEM],
        out_specs=VMEM,
        compiler_params=pltpu.CompilerParams(vmem_limit_bytes=8 << 20),
    )(table, scattered.reshape(pieces * blocks, sub, width))
    if cap < sib * blocks:
        right = turned(own, "col_x", 1)
        left = turned(own, "col_x", -1)
        beside = swapped(own, "col_y", 1)
        right_beside = turned(beside, "col_x", 1)
        left_beside = turned(beside, "col_x", -1)
        right_two = turned(right, "col_x", 1)
        left_two = turned(left_beside, "col_x", -1)
        g0 = jnp.stack([own, beside, right, left])
        g1 = jnp.stack([right_beside, left_beside, right_two, left_two])
        c0 = swapped(g0, "core", 1)
        c1 = swapped(g1, "core", 1)
    else:
        all_pieces = lax.all_to_all(
            jnp.broadcast_to(own[None], (pieces, *own.shape)), COL, 0, 0, tiled=True
        )
        order = piece_columns()
        parts = jnp.concatenate(
            [lax.dynamic_index_in_dim(all_pieces, order[i], 0) for i in range(pieces)]
        )
        g0, g1, c0, c1 = (parts[i : i + 4] for i in range(0, pieces, 4))
    chunk = width // near_chunks
    u, p_hi, p_lo = pl.pallas_call(
        functools.partial(product_kernel, cap, sib),
        out_shape=(
            jax.ShapeDtypeStruct((near_chunks, cap, chunk, BLK), jnp.float32),
            jax.ShapeDtypeStruct((cap, BLK, width), jnp.bfloat16),
            jax.ShapeDtypeStruct((cap, BLK, width), jnp.bfloat16),
        ),
        in_specs=[SMEM] + [VMEM] * 6,
        out_specs=(VMEM, VMEM, VMEM),
        scratch_shapes=[
            pltpu.VMEM((cap, BLK, width), jnp.float32),
            pltpu.VMEM((row_cells // BLK // 2, width, 6 * BLK), jnp.bfloat16),
            pltpu.VMEM((width, 2 * BLK), jnp.float32),
        ],
        compiler_params=pltpu.CompilerParams(vmem_limit_bytes=40 << 20),
    )(table, g0, g1, c0, c1, a_hi, a_lo)
    z = lax.axis_index("row_0")
    if cap < sib * blocks:
        bounds = [0, 8, cap // 2, cap // 2 + 9, cap]
        strands = []
        for first, last, way in zip(bounds, bounds[1:], (1, 1, -1, -1)):
            strands.append((first, last, way, ring_term(u, z - way, first, last)))
        for step in range(1, near_chunks):
            strands = [
                (
                    first,
                    last,
                    way,
                    turned(x, "row_0", way) + ring_term(u, z - way * (1 + step), first, last),
                )
                for first, last, way, x in strands
            ]
        near = [x for _, _, _, x in strands]
    else:
        near = [jnp.sum(lax.all_to_all(u, "row_0", 0, 0, tiled=True), axis=0)]
    half = lax.axis_index("row_1")
    sent = halves(near, 1 - half, half_rows)
    total = halves(near, half, half_rows) + swapped(sent, "row_1", 1)
    unpack = lambda base, x: pl.pallas_call(
        functools.partial(unpack_kernel, base),
        out_shape=jax.ShapeDtypeStruct((sib, half_rows, col_cells), jnp.float32),
        in_specs=[SMEM, VMEM],
        out_specs=VMEM,
        compiler_params=pltpu.CompilerParams(vmem_limit_bytes=8 << 20),
        cost_estimate=pl.CostEstimate(flops=0, transcendentals=0, bytes_accessed=1 << 20),
    )(table, x)
    upper_part = unpack(COL_SLOT, total)
    n_row = lax.axis_size(ROW)
    n_col = lax.axis_size(COL)
    spots = [(r, c) for r in range(n_row) for c in range(n_col)]
    across = [(r * n_col + c, r * n_col + (-r - c) % n_col) for r, c in spots]
    along = [(r * n_col + k, (-r - k) % n_row * n_col + k) for r, k in spots]
    moved = lax.ppermute(lax.ppermute(total, ROW + COL, across), ROW + COL, along)
    inner = pl.pallas_call(
        functools.partial(inner_kernel, sib),
        out_shape=jax.ShapeDtypeStruct((sib, half_rows, width), jnp.float32),
        in_specs=[SMEM] + [VMEM] * 3,
        out_specs=VMEM,
        compiler_params=pltpu.CompilerParams(vmem_limit_bytes=12 << 20),
    )(table, moved, p_hi, p_lo)
    return upper_part, unpack(ROW_SLOT, moved), inner


def piece_columns():
    y = lax.axis_index("col_y")
    x = lax.axis_index("col_x")
    core = lax.axis_index("core")
    n_x = lax.axis_size("col_x")
    places = [(y, x), (1 - y, x), (y, x - 1), (y, x + 1)]
    places += [(1 - y, x - 1), (1 - y, x + 1), (y, x - 2), (1 - y, x + 2)]
    return jnp.stack(
        [
            (py * n_x + (px + n_x) % n_x) * 2 + pc
            for pc in (core, 1 - core)
            for py, px in places
        ]
    ).astype(jnp.int32)


def per_device(anc_inverse, l_store, diag_inv, block_lists, block_counts, sibling_columns):
    row_cells, col_cells = anc_inverse.shape
    width = l_store.shape[2]
    sib = sibling_columns.shape[0]
    n_col = lax.axis_size(COL)
    n_row = lax.axis_size(ROW)
    row_index = lax.axis_index(ROW)
    col_index = lax.axis_index(COL)
    blocks = row_cells // BLK
    cut = l_store[0].reshape(blocks, n_col, SUB, width).transpose(1, 0, 2, 3)
    scattered = lax.all_to_all(cut, COL, 0, 0, tiled=True)
    rounded = lax.reduce_precision(anc_inverse, 8, 7)
    a_hi = rounded.astype(jnp.bfloat16)
    a_lo = (anc_inverse - rounded).astype(jnp.bfloat16)

    listed = member_blocks(block_lists, block_counts, n_row * blocks)
    groups = listed.reshape(sib, n_row, blocks)
    most = jnp.max(jnp.sum(groups, axis=(0, 2)))
    row_code, row_start, row_slot = slot_tables(
        lax.dynamic_index_in_dim(groups, row_index, 1, keepdims=False)
    )
    col_code, col_start, col_slot = slot_tables(
        lax.dynamic_index_in_dim(groups, col_index, 1, keepdims=False)
    )
    owner = jnp.sum(
        jnp.where(
            (row_code // blocks)[:, None] == jnp.arange(sib, dtype=jnp.int32)[None, :],
            sibling_columns[None, :],
            0,
        ),
        axis=1,
    )
    table = jnp.concatenate(
        [
            padded(row_code % blocks, 64),
            padded(row_start, 8),
            padded(col_code % blocks, 64),
            padded(col_start, 8),
            padded(piece_columns(), 16),
            padded(row_slot, 64),
            padded(col_slot, 64),
            padded(owner * blocks + row_code % blocks, 64),
            padded(sibling_columns, 8),
            jnp.stack([jnp.any(sibling_columns == col_index).astype(jnp.int32), row_index]),
        ]
    )
    caps = [c for c in CAPS if c < sib * blocks] + [sib * blocks]
    which = sum((most > c).astype(jnp.int32) for c in caps[:-1])
    upper_part, moved, inner = lax.switch(
        which,
        [functools.partial(listed_products, c, sib) for c in caps],
        table,
        scattered,
        a_hi,
        a_lo,
    )
    for bit in (1, 4):
        others = []
        for away in (bit, 2 * bit, 3 * bit):
            pairs = [
                (r * n_col + k, (r ^ away) * n_col + (k + r - (r ^ away)) % n_col)
                for r in range(n_row)
                for k in range(n_col)
            ]
            others.append(lax.ppermute(inner, ROW + COL, pairs))
        inner = (inner + others[0]) + (others[1] + others[2])
    slots = pl.pallas_call(
        slots_kernel,
        out_shape=jax.ShapeDtypeStruct((n_col, width // n_row, row_cells + width), jnp.float32),
        in_specs=[SMEM] + [VMEM] * 2,
        out_specs=VMEM,
        compiler_params=pltpu.CompilerParams(vmem_limit_bytes=8 << 20),
    )(table, moved, inner)
    gathered = lax.all_to_all(slots, COL, 0, 0, tiled=True)
    lower, diag = pl.pallas_call(
        finish_kernel,
        out_shape=(
            jax.ShapeDtypeStruct((row_cells, width), jnp.float32),
            jax.ShapeDtypeStruct((width, width), jnp.float32),
        ),
        in_specs=[SMEM] + [VMEM] * 2,
        out_specs=(VMEM, VMEM),
        compiler_params=pltpu.CompilerParams(vmem_limit_bytes=12 << 20),
    )(table, gathered, diag_inv[0])
    return (upper_part, lower[None], diag[None])


def solution(mesh):
    finer = Mesh(mesh.devices.reshape(8, 2, 2, 4, 2), ROW + COL)
    return jax.shard_map(
        per_device,
        mesh=finer,
        in_specs=(P(ROW, COL), P(COL, ROW, None), P(COL, None, None), P(), P(), P()),
        out_specs=(P(None, ROW, COL), P(COL, ROW, None), P(COL, None, None)),
        check_vma=False,
    )
```

```python
import functools

import jax
import jax.numpy as jnp
from jax import lax
from jax.experimental import pallas as pl
from jax.experimental.pallas import tpu as pltpu
from jax.sharding import Mesh
from jax.sharding import PartitionSpec as P

BLK = 128
SUB = 8
ROW = ("row_0", "row_1")
COL = ("col_y", "col_x", "core")
CAPS = (28,)

ROW_BLOCK, ROW_START, COL_BLOCK, COL_START = 0, 64, 72, 136
PIECE, ROW_SLOT, COL_SLOT, SOURCE, OWNER, PRESENT, AT_ROW = 144, 160, 224, 288, 352, 360, 361

SMEM = pl.BlockSpec(memory_space=pltpu.SMEM)
VMEM = pl.BlockSpec(memory_space=pltpu.VMEM)


def swapped(x, axis, bit):
    length = lax.axis_size(axis)
    return lax.ppermute(x, axis, [(i, i ^ bit) for i in range(length)])


def turned(x, axis, shift):
    length = lax.axis_size(axis)
    return lax.ppermute(x, axis, [(i, (i + shift) % length) for i in range(length)])


def member_blocks(block_lists, block_counts, block_total):
    block_ids = jnp.arange(block_total, dtype=jnp.int32)
    valid_entry = jnp.arange(block_lists.shape[1], dtype=jnp.int32)[None, :] < block_counts[:, None]
    entry_hits = (block_lists[:, :, None] == block_ids[None, None, :]) & valid_entry[:, :, None]
    return jnp.any(entry_hits, axis=1).astype(jnp.int32)


def slot_tables(listed):
    sib, blocks = listed.shape
    flat = listed.reshape(-1)
    place = jnp.arange(sib * blocks, dtype=jnp.int32)
    before = jnp.sum(jnp.where(place[None, :] < place[:, None], flat[None, :], 0), axis=1)
    here = (before[None, :] == place[:, None]) & (flat[None, :] > 0)
    code = jnp.sum(jnp.where(here, place[None, :], 0), axis=1)
    bounds = jnp.arange(sib + 1, dtype=jnp.int32) * blocks
    start = jnp.sum(jnp.where(place[None, :] < bounds[:, None], flat[None, :], 0), axis=1)
    slot = jnp.where(flat > 0, before, -1)
    return code, start, slot


def padded(values, length):
    return jnp.pad(values.astype(jnp.int32), (0, length - values.shape[0]))


def pick_kernel(cap, tab, x_ref, o_ref):
    def one(q, carry):
        o_ref[q] = x_ref[tab[SOURCE + q]]
        return carry

    lax.fori_loop(0, cap, one, 0)


def product_kernel(cap, sib, tab, g0, g1, c0, c1, ah, al, u_ref, ph_ref, pl_ref, p_ref, lhs, acc):
    parts = (g0, g1, c0, c1)
    for i in range(4 * len(parts)):
        at = pl.multiple_of(tab[PIECE + i] * SUB, SUB)
        p_ref[:, pl.ds(at, SUB), :] = parts[i // 4][i % 4]
    chunks, _, rows, _ = u_ref.shape

    def tile(ref, b, t):
        return ref[
            pl.ds(pl.multiple_of(b * BLK, BLK), BLK), pl.ds(pl.multiple_of(t * BLK, BLK), BLK)
        ]

    def square(ref, b0, b1, t0, t1):
        top = jnp.concatenate([tile(ref, b0, t0), tile(ref, b0, t1)], axis=1)
        low = jnp.concatenate([tile(ref, b1, t0), tile(ref, b1, t1)], axis=1)
        return jnp.concatenate([top, low], axis=0)

    def sibling(j, outer):
        r0 = tab[ROW_START + j]
        r1 = tab[ROW_START + j + 1]
        n0 = tab[COL_START + j]
        n1 = tab[COL_START + j + 1]
        quads = (r1 - r0 + 3) // 4

        def listed_panel(q):
            return jnp.where(q < r1, p_ref[jnp.minimum(q, cap - 1)], 0.0)

        def split(i, carry):
            q = r0 + 2 * i
            block = jnp.concatenate([listed_panel(q), listed_panel(q + 1)], axis=0)
            hi = block.astype(jnp.bfloat16)
            lo = (block - hi.astype(jnp.float32)).astype(jnp.bfloat16)

            @pl.when(q < r1)
            def _():
                ph_ref[q] = hi[:BLK]
                pl_ref[q] = lo[:BLK]

            @pl.when(q + 1 < r1)
            def _():
                ph_ref[q + 1] = hi[BLK:]
                pl_ref[q + 1] = lo[BLK:]

            across = hi.T
            lhs[i] = jnp.concatenate([across, across, lo.T], axis=1)
            return carry

        lax.fori_loop(0, 2 * quads, split, 0)

        def columns(o, carry):
            s = n0 + 2 * o
            t0 = tab[COL_BLOCK + s]
            t1 = tab[COL_BLOCK + s + 1]
            acc[...] = jnp.zeros_like(acc)

            def rows_of(i, inner):
                terms = []
                for k in range(2):
                    b0 = tab[ROW_BLOCK + r0 + 4 * i + 2 * k]
                    b1 = tab[ROW_BLOCK + r0 + 4 * i + 2 * k + 1]
                    hi = square(ah, b0, b1, t0, t1)
                    lo = square(al, b0, b1, t0, t1)
                    terms.append(
                        jnp.dot(
                            lhs[2 * i + k],
                            jnp.concatenate([hi, lo, hi], axis=0),
                            preferred_element_type=jnp.float32,
                        )
                    )
                acc[...] += terms[0] + terms[1]
                return inner

            lax.fori_loop(0, quads, rows_of, 0)
            for z in range(chunks):
                u_ref[z, s] = -acc[z * rows : (z + 1) * rows, :BLK]

            @pl.when(s + 1 < n1)
            def _():
                for z in range(chunks):
                    u_ref[z, s + 1] = -acc[z * rows : (z + 1) * rows, BLK:]

            return carry

        lax.fori_loop(0, (n1 - n0 + 1) // 2, columns, 0)
        return outer

    if cap < sib * (ah.shape[0] // BLK):
        for j in range(sib):
            sibling(j, 0)
    else:
        lax.fori_loop(0, sib, sibling, 0)

    def clear(s, carry):
        u_ref[:, s] = jnp.zeros((chunks, rows, BLK), jnp.float32)
        return carry

    lax.fori_loop(tab[COL_START + sib], cap, clear, 0)


def unpack_kernel(base, tab, x_ref, o_ref):
    sib, _, cells = o_ref.shape
    blocks = cells // BLK

    def sibling(j, carry):
        for b in range(blocks):
            slot = tab[base + j * blocks + b]
            o_ref[j, :, b * BLK : (b + 1) * BLK] = jnp.where(
                slot >= 0, x_ref[jnp.maximum(slot, 0)], 0.0
            )
        return carry

    lax.fori_loop(0, sib, sibling, 0)


def inner_kernel(sib, tab, x_ref, hi_ref, lo_ref, o_ref):
    def sibling(j, carry):
        def one(q, total):
            x = x_ref[q]
            x_hi = x.astype(jnp.bfloat16)
            x_lo = (x - x_hi.astype(jnp.float32)).astype(jnp.bfloat16)
            hi = hi_ref[q]
            return total + jnp.dot(
                jnp.concatenate([x_hi, x_lo, x_hi], axis=1),
                jnp.concatenate([hi, hi, lo_ref[q]], axis=0),
                preferred_element_type=jnp.float32,
            )

        o_ref[j] = lax.fori_loop(
            tab[ROW_START + j],
            tab[ROW_START + j + 1],
            one,
            jnp.zeros(o_ref.shape[1:], jnp.float32),
        )
        return carry

    lax.fori_loop(0, sib, sibling, 0)


def slots_kernel(tab, x_ref, inner_ref, o_ref):
    sib, _, cells = x_ref.shape

    def clear(d, carry):
        o_ref[d] = jnp.zeros(o_ref.shape[1:], jnp.float32)
        return carry

    lax.fori_loop(0, o_ref.shape[0], clear, 0)
    for j in range(sib):
        at = tab[OWNER + j]
        o_ref[at, :, :cells] = x_ref[j]
        o_ref[at, :, cells:] = inner_ref[j]


def finish_kernel(tab, x_ref, diag_ref, lower_ref, out_ref):
    n_row = x_ref.shape[0]
    cells = lower_ref.shape[0]
    places = [lax.rem(2 * n_row - r - tab[AT_ROW], n_row) for r in range(n_row)]
    for b in range(cells // BLK):
        stack = jnp.concatenate([x_ref[p, :, b * BLK : (b + 1) * BLK] for p in places], axis=0)
        lower_ref[b * BLK : (b + 1) * BLK, :] = stack.T
    total = jnp.concatenate([x_ref[p, :, cells:] for p in places], axis=0)
    out_ref[...] = jnp.where(tab[PRESENT] > 0, diag_ref[...] - total, 0.0)


def ring_term(u, z, first, last, lead):
    part = lax.dynamic_index_in_dim(u, (z + 2 * u.shape[0]) % u.shape[0], 0, keepdims=False)
    part = part[first:last]
    return part if lead == 1 else part.reshape(lead, -1, *part.shape[1:])


def halves(parts, half, rows):
    return jnp.concatenate([lax.dynamic_slice_in_dim(x, half * rows, rows, 1) for x in parts])


def listed_products(cap, sib, table, scattered, a_hi, a_lo):
    row_cells, col_cells = a_hi.shape
    pieces, blocks, sub, width = scattered.shape
    near_chunks = lax.axis_size("row_0")
    half_rows = width // (near_chunks * lax.axis_size("row_1"))
    own = pl.pallas_call(
        functools.partial(pick_kernel, cap),
        out_shape=jax.ShapeDtypeStruct((cap, sub, width), jnp.float32),
        in_specs=[SMEM, VMEM],
        out_specs=VMEM,
        compiler_params=pltpu.CompilerParams(vmem_limit_bytes=8 << 20),
    )(table, scattered.reshape(pieces * blocks, sub, width))
    if cap < sib * blocks:
        right = turned(own, "col_x", 1)
        left = turned(own, "col_x", -1)
        beside = swapped(own, "col_y", 1)
        right_beside = turned(beside, "col_x", 1)
        left_beside = turned(beside, "col_x", -1)
        right_two = turned(right, "col_x", 1)
        left_two = turned(left_beside, "col_x", -1)
        g0 = jnp.stack([own, beside, right, left])
        g1 = jnp.stack([right_beside, left_beside, right_two, left_two])
        c0 = swapped(g0, "core", 1)
        c1 = swapped(g1, "core", 1)
    else:
        all_pieces = lax.all_to_all(
            jnp.broadcast_to(own[None], (pieces, *own.shape)), COL, 0, 0, tiled=True
        )
        order = piece_columns()
        parts = jnp.concatenate(
            [lax.dynamic_index_in_dim(all_pieces, order[i], 0) for i in range(pieces)]
        )
        g0, g1, c0, c1 = (parts[i : i + 4] for i in range(0, pieces, 4))
    chunk = width // near_chunks
    u, p_hi, p_lo = pl.pallas_call(
        functools.partial(product_kernel, cap, sib),
        out_shape=(
            jax.ShapeDtypeStruct((near_chunks, cap, chunk, BLK), jnp.float32),
            jax.ShapeDtypeStruct((cap, BLK, width), jnp.bfloat16),
            jax.ShapeDtypeStruct((cap, BLK, width), jnp.bfloat16),
        ),
        in_specs=[SMEM] + [VMEM] * 6,
        out_specs=(VMEM, VMEM, VMEM),
        scratch_shapes=[
            pltpu.VMEM((cap, BLK, width), jnp.float32),
            pltpu.VMEM((row_cells // BLK // 2 + 1, width, 6 * BLK), jnp.bfloat16),
            pltpu.VMEM((width, 2 * BLK), jnp.float32),
        ],
        compiler_params=pltpu.CompilerParams(vmem_limit_bytes=40 << 20),
    )(table, g0, g1, c0, c1, a_hi, a_lo)
    z = lax.axis_index("row_0")
    if cap < sib * blocks:
        strands = [(0, cap // 2, 1, 1), (cap // 2, cap, 2, -1)]
        near = [ring_term(u, z - way, first, last, lead) for first, last, lead, way in strands]
        for step in range(1, near_chunks):
            near = [
                turned(x, "row_0", way) + ring_term(u, z - way * (1 + step), first, last, lead)
                for x, (first, last, lead, way) in zip(near, strands)
            ]
        near = [x.reshape(-1, *x.shape[-2:]) for x in near]
    else:
        near = [jnp.sum(lax.all_to_all(u, "row_0", 0, 0, tiled=True), axis=0)]
    half = lax.axis_index("row_1")
    sent = halves(near, 1 - half, half_rows)
    kept = halves(near, half, half_rows)
    n_row = lax.axis_size(ROW)
    n_col = lax.axis_size(COL)
    spots = [(r, c) for r in range(n_row) for c in range(n_col)]
    across = [(r * n_col + c, r * n_col + (-r - c) % n_col) for r, c in spots]
    over = [(r * n_col + c, (r ^ 1) * n_col + (-(r ^ 1) - c) % n_col) for r, c in spots]
    along = [(r * n_col + k, (-r - k) % n_row * n_col + k) for r, k in spots]
    midway = lax.ppermute(kept, ROW + COL, across) + lax.ppermute(sent, ROW + COL, over)
    moved = lax.ppermute(midway, ROW + COL, along)
    total = kept + swapped(sent, "row_1", 1)
    unpack = lambda base, x: pl.pallas_call(
        functools.partial(unpack_kernel, base),
        out_shape=jax.ShapeDtypeStruct((sib, half_rows, col_cells), jnp.float32),
        in_specs=[SMEM, VMEM],
        out_specs=VMEM,
        compiler_params=pltpu.CompilerParams(vmem_limit_bytes=8 << 20),
        cost_estimate=pl.CostEstimate(flops=0, transcendentals=0, bytes_accessed=1 << 20),
    )(table, x)
    upper_part = unpack(COL_SLOT, total)
    inner = pl.pallas_call(
        functools.partial(inner_kernel, sib),
        out_shape=jax.ShapeDtypeStruct((sib, half_rows, width), jnp.float32),
        in_specs=[SMEM] + [VMEM] * 3,
        out_specs=VMEM,
        compiler_params=pltpu.CompilerParams(vmem_limit_bytes=12 << 20),
    )(table, moved, p_hi, p_lo)
    return upper_part, unpack(ROW_SLOT, moved), inner


def piece_columns():
    y = lax.axis_index("col_y")
    x = lax.axis_index("col_x")
    core = lax.axis_index("core")
    n_x = lax.axis_size("col_x")
    places = [(y, x), (1 - y, x), (y, x - 1), (y, x + 1)]
    places += [(1 - y, x - 1), (1 - y, x + 1), (y, x - 2), (1 - y, x + 2)]
    return jnp.stack(
        [
            (py * n_x + (px + n_x) % n_x) * 2 + pc
            for pc in (core, 1 - core)
            for py, px in places
        ]
    ).astype(jnp.int32)


def per_device(anc_inverse, l_store, diag_inv, block_lists, block_counts, sibling_columns):
    row_cells, col_cells = anc_inverse.shape
    width = l_store.shape[2]
    sib = sibling_columns.shape[0]
    n_col = lax.axis_size(COL)
    n_row = lax.axis_size(ROW)
    row_index = lax.axis_index(ROW)
    col_index = lax.axis_index(COL)
    blocks = row_cells // BLK
    cut = l_store[0].reshape(blocks, n_col, SUB, width).transpose(1, 0, 2, 3)
    scattered = lax.all_to_all(cut, COL, 0, 0, tiled=True)
    rounded = lax.reduce_precision(anc_inverse, 8, 7)
    a_hi = rounded.astype(jnp.bfloat16)
    a_lo = (anc_inverse - rounded).astype(jnp.bfloat16)

    listed = member_blocks(block_lists, block_counts, n_row * blocks)
    groups = listed.reshape(sib, n_row, blocks)
    most = jnp.max(jnp.sum(groups, axis=(0, 2)))
    row_code, row_start, row_slot = slot_tables(
        lax.dynamic_index_in_dim(groups, row_index, 1, keepdims=False)
    )
    col_code, col_start, col_slot = slot_tables(
        lax.dynamic_index_in_dim(groups, col_index, 1, keepdims=False)
    )
    owner = jnp.sum(
        jnp.where(
            (row_code // blocks)[:, None] == jnp.arange(sib, dtype=jnp.int32)[None, :],
            sibling_columns[None, :],
            0,
        ),
        axis=1,
    )
    table = jnp.concatenate(
        [
            padded(row_code % blocks, 64),
            padded(row_start, 8),
            padded(col_code % blocks, 64),
            padded(col_start, 8),
            padded(piece_columns(), 16),
            padded(row_slot, 64),
            padded(col_slot, 64),
            padded(owner * blocks + row_code % blocks, 64),
            padded(sibling_columns, 8),
            jnp.stack([jnp.any(sibling_columns == col_index).astype(jnp.int32), row_index]),
        ]
    )
    caps = [c for c in CAPS if c < sib * blocks] + [sib * blocks]
    which = sum((most > c).astype(jnp.int32) for c in caps[:-1])
    upper_part, moved, inner = lax.switch(
        which,
        [functools.partial(listed_products, c, sib) for c in caps],
        table,
        scattered,
        a_hi,
        a_lo,
    )
    for bit in (1, 4):
        others = []
        for away in (bit, 2 * bit, 3 * bit):
            pairs = [
                (r * n_col + k, (r ^ away) * n_col + (k + r - (r ^ away)) % n_col)
                for r in range(n_row)
                for k in range(n_col)
            ]
            others.append(lax.ppermute(inner, ROW + COL, pairs))
        inner = (inner + others[0]) + (others[1] + others[2])
    slots = pl.pallas_call(
        slots_kernel,
        out_shape=jax.ShapeDtypeStruct((n_col, width // n_row, row_cells + width), jnp.float32),
        in_specs=[SMEM] + [VMEM] * 2,
        out_specs=VMEM,
        compiler_params=pltpu.CompilerParams(vmem_limit_bytes=8 << 20),
    )(table, moved, inner)
    gathered = lax.all_to_all(slots, COL, 0, 0, tiled=True)
    lower, diag = pl.pallas_call(
        finish_kernel,
        out_shape=(
            jax.ShapeDtypeStruct((row_cells, width), jnp.float32),
            jax.ShapeDtypeStruct((width, width), jnp.float32),
        ),
        in_specs=[SMEM] + [VMEM] * 2,
        out_specs=(VMEM, VMEM),
        compiler_params=pltpu.CompilerParams(vmem_limit_bytes=12 << 20),
    )(table, gathered, diag_inv[0])
    return (upper_part, lower[None], diag[None])


def solution(mesh):
    finer = Mesh(mesh.devices.reshape(8, 2, 2, 4, 2), ROW + COL)
    return jax.shard_map(
        per_device,
        mesh=finer,
        in_specs=(P(ROW, COL), P(COL, ROW, None), P(COL, None, None), P(), P(), P()),
        out_specs=(P(None, ROW, COL), P(COL, ROW, None), P(COL, None, None)),
        check_vma=False,
    )
```

```python
import functools

import jax
import jax.numpy as jnp
from jax import lax
from jax.experimental import pallas as pl
from jax.experimental.pallas import tpu as pltpu
from jax.sharding import Mesh
from jax.sharding import PartitionSpec as P

BLK = 128
SUB = 8
ROW = ("row_0", "row_1")
COL = ("col_y", "col_x", "core")
CAPS = (28,)

ROW_BLOCK, ROW_START, COL_BLOCK, COL_START = 0, 64, 72, 136
PIECE, ROW_SLOT, COL_SLOT, SOURCE, OWNER, PRESENT, AT_ROW = 144, 160, 224, 288, 352, 360, 361

SMEM = pl.BlockSpec(memory_space=pltpu.SMEM)
VMEM = pl.BlockSpec(memory_space=pltpu.VMEM)


def swapped(x, axis, bit):
    length = lax.axis_size(axis)
    return lax.ppermute(x, axis, [(i, i ^ bit) for i in range(length)])


def turned(x, axis, shift):
    length = lax.axis_size(axis)
    return lax.ppermute(x, axis, [(i, (i + shift) % length) for i in range(length)])


def member_blocks(block_lists, block_counts, block_total):
    block_ids = jnp.arange(block_total, dtype=jnp.int32)
    valid_entry = jnp.arange(block_lists.shape[1], dtype=jnp.int32)[None, :] < block_counts[:, None]
    entry_hits = (block_lists[:, :, None] == block_ids[None, None, :]) & valid_entry[:, :, None]
    return jnp.any(entry_hits, axis=1).astype(jnp.int32)


def slot_tables(listed):
    sib, blocks = listed.shape
    flat = listed.reshape(-1)
    place = jnp.arange(sib * blocks, dtype=jnp.int32)
    before = jnp.sum(jnp.where(place[None, :] < place[:, None], flat[None, :], 0), axis=1)
    here = (before[None, :] == place[:, None]) & (flat[None, :] > 0)
    code = jnp.sum(jnp.where(here, place[None, :], 0), axis=1)
    bounds = jnp.arange(sib + 1, dtype=jnp.int32) * blocks
    start = jnp.sum(jnp.where(place[None, :] < bounds[:, None], flat[None, :], 0), axis=1)
    slot = jnp.where(flat > 0, before, -1)
    return code, start, slot


def padded(values, length):
    return jnp.pad(values.astype(jnp.int32), (0, length - values.shape[0]))


def pick_kernel(cap, tab, x_ref, o_ref):
    def one(q, carry):
        o_ref[q] = x_ref[tab[SOURCE + q]]
        return carry

    lax.fori_loop(0, cap, one, 0)


def product_kernel(cap, sib, tab, g0, g1, c0, c1, ah, al, u_ref, ph_ref, pl_ref, p_ref, lhs, acc):
    parts = (g0, g1, c0, c1)
    fast = cap < sib * (ah.shape[0] // BLK)
    for i in range(4 * len(parts)):
        at = pl.multiple_of(tab[PIECE + i] * SUB, SUB) if fast else i * SUB
        p_ref[:, pl.ds(at, SUB), :] = parts[i // 4][i % 4]
    chunks, _, rows, _ = u_ref.shape

    def tile(ref, b, t):
        return ref[
            pl.ds(pl.multiple_of(b * BLK, BLK), BLK), pl.ds(pl.multiple_of(t * BLK, BLK), BLK)
        ]

    def square(ref, b0, b1, t0, t1):
        top = jnp.concatenate([tile(ref, b0, t0), tile(ref, b0, t1)], axis=1)
        low = jnp.concatenate([tile(ref, b1, t0), tile(ref, b1, t1)], axis=1)
        return jnp.concatenate([top, low], axis=0)

    def sibling(j, outer):
        r0 = tab[ROW_START + j]
        r1 = tab[ROW_START + j + 1]
        n0 = tab[COL_START + j]
        n1 = tab[COL_START + j + 1]
        quads = (r1 - r0 + 3) // 4

        def listed_panel(q):
            return jnp.where(q < r1, p_ref[jnp.minimum(q, cap - 1)], 0.0)

        def split(i, carry):
            q = r0 + 2 * i
            block = jnp.concatenate([listed_panel(q), listed_panel(q + 1)], axis=0)
            hi = block.astype(jnp.bfloat16)
            lo = (block - hi.astype(jnp.float32)).astype(jnp.bfloat16)

            @pl.when(q < r1)
            def _():
                ph_ref[q] = hi[:BLK]
                pl_ref[q] = lo[:BLK]

            @pl.when(q + 1 < r1)
            def _():
                ph_ref[q + 1] = hi[BLK:]
                pl_ref[q + 1] = lo[BLK:]

            across = hi.T
            lhs[i] = jnp.concatenate([across, across, lo.T], axis=1)
            return carry

        lax.fori_loop(0, 2 * quads, split, 0)

        def columns(o, carry):
            s = n0 + 2 * o
            t0 = tab[COL_BLOCK + s]
            t1 = tab[COL_BLOCK + s + 1]
            acc[...] = jnp.zeros_like(acc)

            def rows_of(i, inner):
                terms = []
                for k in range(2):
                    b0 = tab[ROW_BLOCK + r0 + 4 * i + 2 * k]
                    b1 = tab[ROW_BLOCK + r0 + 4 * i + 2 * k + 1]
                    hi = square(ah, b0, b1, t0, t1)
                    lo = square(al, b0, b1, t0, t1)
                    terms.append(
                        jnp.dot(
                            lhs[2 * i + k],
                            jnp.concatenate([hi, lo, hi], axis=0),
                            preferred_element_type=jnp.float32,
                        )
                    )
                acc[...] += terms[0] + terms[1]
                return inner

            lax.fori_loop(0, quads, rows_of, 0)
            for z in range(chunks):
                u_ref[z, s] = -acc[z * rows : (z + 1) * rows, :BLK]

            @pl.when(s + 1 < n1)
            def _():
                for z in range(chunks):
                    u_ref[z, s + 1] = -acc[z * rows : (z + 1) * rows, BLK:]

            return carry

        lax.fori_loop(0, (n1 - n0 + 1) // 2, columns, 0)
        return outer

    if fast:
        for j in range(sib):
            sibling(j, 0)
    else:
        lax.fori_loop(0, sib, sibling, 0)

    def clear(s, carry):
        u_ref[:, s] = jnp.zeros((chunks, rows, BLK), jnp.float32)
        return carry

    lax.fori_loop(tab[COL_START + sib], cap, clear, 0)


def unpack_kernel(base, tab, x_ref, o_ref):
    sib, _, cells = o_ref.shape
    blocks = cells // BLK

    def sibling(j, carry):
        for b in range(blocks):
            slot = tab[base + j * blocks + b]
            o_ref[j, :, b * BLK : (b + 1) * BLK] = jnp.where(
                slot >= 0, x_ref[jnp.maximum(slot, 0)], 0.0
            )
        return carry

    lax.fori_loop(0, sib, sibling, 0)


def inner_kernel(sib, tab, x_ref, hi_ref, lo_ref, o_ref):
    def sibling(j, carry):
        def one(q, total):
            x = x_ref[q]
            x_hi = x.astype(jnp.bfloat16)
            x_lo = (x - x_hi.astype(jnp.float32)).astype(jnp.bfloat16)
            hi = hi_ref[q]
            return total + jnp.dot(
                jnp.concatenate([x_hi, x_lo, x_hi], axis=1),
                jnp.concatenate([hi, hi, lo_ref[q]], axis=0),
                preferred_element_type=jnp.float32,
            )

        o_ref[j] = lax.fori_loop(
            tab[ROW_START + j],
            tab[ROW_START + j + 1],
            one,
            jnp.zeros(o_ref.shape[1:], jnp.float32),
        )
        return carry

    lax.fori_loop(0, sib, sibling, 0)


def place_kernel(tab, x_ref, o_ref):
    sib = x_ref.shape[0]

    def clear(d, carry):
        o_ref[d] = jnp.zeros(o_ref.shape[1:], jnp.float32)
        return carry

    lax.fori_loop(0, o_ref.shape[0], clear, 0)
    for j in range(sib):
        o_ref[tab[OWNER + j]] = x_ref[j]


def source_columns(tab, n_row):
    return [lax.rem(2 * n_row - r - tab[AT_ROW], n_row) for r in range(n_row)]


def lower_kernel(tab, x_ref, lower_ref):
    places = source_columns(tab, x_ref.shape[0])
    for b in range(lower_ref.shape[0] // BLK):
        stack = jnp.concatenate([x_ref[p, :, b * BLK : (b + 1) * BLK] for p in places], axis=0)
        lower_ref[b * BLK : (b + 1) * BLK, :] = stack.T


def diag_kernel(tab, x_ref, diag_ref, out_ref):
    total = jnp.concatenate([x_ref[p] for p in source_columns(tab, x_ref.shape[0])], axis=0)
    out_ref[...] = jnp.where(tab[PRESENT] > 0, diag_ref[...] - total, 0.0)


def ring_term(u, z, first, last, lead):
    part = lax.dynamic_index_in_dim(u, (z + 2 * u.shape[0]) % u.shape[0], 0, keepdims=False)
    part = part[first:last]
    return part if lead == 1 else part.reshape(lead, -1, *part.shape[1:])


def halves(parts, half, rows):
    return jnp.concatenate([lax.dynamic_slice_in_dim(x, half * rows, rows, 1) for x in parts])


def listed_products(cap, sib, table, scattered, a_hi, a_lo):
    row_cells, col_cells = a_hi.shape
    pieces, blocks, sub, width = scattered.shape
    near_chunks = lax.axis_size("row_0")
    half_rows = width // (near_chunks * lax.axis_size("row_1"))
    own = pl.pallas_call(
        functools.partial(pick_kernel, cap),
        out_shape=jax.ShapeDtypeStruct((cap, sub, width), jnp.float32),
        in_specs=[SMEM, VMEM],
        out_specs=VMEM,
        compiler_params=pltpu.CompilerParams(vmem_limit_bytes=8 << 20),
    )(table, scattered.reshape(pieces * blocks, sub, width))
    if cap < sib * blocks:
        right = turned(own, "col_x", 1)
        left = turned(own, "col_x", -1)
        beside = swapped(own, "col_y", 1)
        right_beside = turned(beside, "col_x", 1)
        left_beside = turned(beside, "col_x", -1)
        right_two = turned(right, "col_x", 1)
        left_two = turned(left_beside, "col_x", -1)
        g0 = jnp.stack([own, beside, right, left])
        g1 = jnp.stack([right_beside, left_beside, right_two, left_two])
        c0 = swapped(g0, "core", 1)
        c1 = swapped(g1, "core", 1)
    else:
        all_pieces = lax.all_to_all(
            jnp.broadcast_to(own[None], (pieces, *own.shape)), COL, 0, 0, tiled=True
        )
        g0, g1, c0, c1 = (all_pieces[i : i + 4] for i in range(0, pieces, 4))
    chunk = width // near_chunks
    u, p_hi, p_lo = pl.pallas_call(
        functools.partial(product_kernel, cap, sib),
        out_shape=(
            jax.ShapeDtypeStruct((near_chunks, cap, chunk, BLK), jnp.float32),
            jax.ShapeDtypeStruct((cap, BLK, width), jnp.bfloat16),
            jax.ShapeDtypeStruct((cap, BLK, width), jnp.bfloat16),
        ),
        in_specs=[SMEM] + [VMEM] * 6,
        out_specs=(VMEM, VMEM, VMEM),
        scratch_shapes=[
            pltpu.VMEM((cap, BLK, width), jnp.float32),
            pltpu.VMEM((row_cells // BLK // 2 + 1, width, 6 * BLK), jnp.bfloat16),
            pltpu.VMEM((width, 2 * BLK), jnp.float32),
        ],
        compiler_params=pltpu.CompilerParams(vmem_limit_bytes=(26 if cap < sib * blocks else 34) << 20),
    )(table, g0, g1, c0, c1, a_hi, a_lo)
    z = lax.axis_index("row_0")
    if cap < sib * blocks:
        strands = [(0, cap // 2, 1, 1), (cap // 2, cap, 2, -1)]
        near = [ring_term(u, z - way, first, last, lead) for first, last, lead, way in strands]
        for step in range(1, near_chunks):
            near = [
                turned(x, "row_0", way) + ring_term(u, z - way * (1 + step), first, last, lead)
                for x, (first, last, lead, way) in zip(near, strands)
            ]
        near = [x.reshape(-1, *x.shape[-2:]) for x in near]
    else:
        near = [jnp.sum(lax.all_to_all(u, "row_0", 0, 0, tiled=True), axis=0)]
    half = lax.axis_index("row_1")
    sent = halves(near, 1 - half, half_rows)
    kept = halves(near, half, half_rows)
    n_row = lax.axis_size(ROW)
    n_col = lax.axis_size(COL)
    spots = [(r, c) for r in range(n_row) for c in range(n_col)]
    across = [(r * n_col + c, r * n_col + (-r - c) % n_col) for r, c in spots]
    over = [(r * n_col + c, (r ^ 1) * n_col + (-(r ^ 1) - c) % n_col) for r, c in spots]
    along = [(r * n_col + k, (-r - k) % n_row * n_col + k) for r, k in spots]
    midway = lax.ppermute(kept, ROW + COL, across) + lax.ppermute(sent, ROW + COL, over)
    moved = lax.ppermute(midway, ROW + COL, along)
    total = kept + swapped(sent, "row_1", 1)
    unpack = lambda base, x: pl.pallas_call(
        functools.partial(unpack_kernel, base),
        out_shape=jax.ShapeDtypeStruct((sib, half_rows, col_cells), jnp.float32),
        in_specs=[SMEM, VMEM],
        out_specs=VMEM,
        compiler_params=pltpu.CompilerParams(vmem_limit_bytes=8 << 20),
        cost_estimate=pl.CostEstimate(flops=0, transcendentals=0, bytes_accessed=1 << 20),
    )(table, x)
    upper_part = unpack(COL_SLOT, total)
    inner = pl.pallas_call(
        functools.partial(inner_kernel, sib),
        out_shape=jax.ShapeDtypeStruct((sib, half_rows, width), jnp.float32),
        in_specs=[SMEM] + [VMEM] * 3,
        out_specs=VMEM,
        compiler_params=pltpu.CompilerParams(vmem_limit_bytes=12 << 20),
    )(table, moved, p_hi, p_lo)
    return upper_part, unpack(ROW_SLOT, moved), inner


def piece_columns():
    y = lax.axis_index("col_y")
    x = lax.axis_index("col_x")
    core = lax.axis_index("core")
    n_x = lax.axis_size("col_x")
    places = [(y, x), (1 - y, x), (y, x - 1), (y, x + 1)]
    places += [(1 - y, x - 1), (1 - y, x + 1), (y, x - 2), (1 - y, x + 2)]
    return jnp.stack(
        [
            (py * n_x + (px + n_x) % n_x) * 2 + pc
            for pc in (core, 1 - core)
            for py, px in places
        ]
    ).astype(jnp.int32)


def per_device(anc_inverse, l_store, diag_inv, block_lists, block_counts, sibling_columns):
    row_cells, col_cells = anc_inverse.shape
    width = l_store.shape[2]
    sib = sibling_columns.shape[0]
    n_col = lax.axis_size(COL)
    n_row = lax.axis_size(ROW)
    row_index = lax.axis_index(ROW)
    col_index = lax.axis_index(COL)
    blocks = row_cells // BLK
    cut = l_store[0].reshape(blocks, n_col, SUB, width).transpose(1, 0, 2, 3)
    scattered = lax.all_to_all(cut, COL, 0, 0, tiled=True)
    rounded = lax.reduce_precision(anc_inverse, 8, 7)
    a_hi = rounded.astype(jnp.bfloat16)
    a_lo = (anc_inverse - rounded).astype(jnp.bfloat16)

    listed = member_blocks(block_lists, block_counts, n_row * blocks)
    groups = listed.reshape(sib, n_row, blocks)
    most = jnp.max(jnp.sum(groups, axis=(0, 2)))
    row_code, row_start, row_slot = slot_tables(
        lax.dynamic_index_in_dim(groups, row_index, 1, keepdims=False)
    )
    col_code, col_start, col_slot = slot_tables(
        lax.dynamic_index_in_dim(groups, col_index, 1, keepdims=False)
    )
    owner = jnp.sum(
        jnp.where(
            (row_code // blocks)[:, None] == jnp.arange(sib, dtype=jnp.int32)[None, :],
            sibling_columns[None, :],
            0,
        ),
        axis=1,
    )
    table = jnp.concatenate(
        [
            padded(row_code % blocks, 64),
            padded(row_start, 8),
            padded(col_code % blocks, 64),
            padded(col_start, 8),
            padded(piece_columns(), 16),
            padded(row_slot, 64),
            padded(col_slot, 64),
            padded(owner * blocks + row_code % blocks, 64),
            padded(sibling_columns, 8),
            jnp.stack([jnp.any(sibling_columns == col_index).astype(jnp.int32), row_index]),
        ]
    )
    caps = [c for c in CAPS if c < sib * blocks] + [sib * blocks]
    which = sum((most > c).astype(jnp.int32) for c in caps[:-1])
    upper_part, moved, inner = lax.switch(
        which,
        [functools.partial(listed_products, c, sib) for c in caps],
        table,
        scattered,
        a_hi,
        a_lo,
    )
    place = lambda x: pl.pallas_call(
        place_kernel,
        out_shape=jax.ShapeDtypeStruct((n_col, *x.shape[1:]), jnp.float32),
        in_specs=[SMEM, VMEM],
        out_specs=VMEM,
        compiler_params=pltpu.CompilerParams(vmem_limit_bytes=8 << 20),
    )(table, x)
    gathered = lax.all_to_all(place(moved), COL, 0, 0, tiled=True)
    for bit in (1, 4):
        others = []
        for away in (bit, 2 * bit, 3 * bit):
            pairs = [
                (r * n_col + k, (r ^ away) * n_col + (k + r - (r ^ away)) % n_col)
                for r in range(n_row)
                for k in range(n_col)
            ]
            others.append(lax.ppermute(inner, ROW + COL, pairs))
        inner = (inner + others[0]) + (others[1] + others[2])
    gathered, inner = lax.optimization_barrier((gathered, inner))
    parts = lax.all_to_all(place(inner), COL, 0, 0, tiled=True)
    lower = pl.pallas_call(
        lower_kernel,
        out_shape=jax.ShapeDtypeStruct((row_cells, width), jnp.float32),
        in_specs=[SMEM, VMEM],
        out_specs=VMEM,
        compiler_params=pltpu.CompilerParams(vmem_limit_bytes=8 << 20),
        cost_estimate=pl.CostEstimate(flops=0, transcendentals=0, bytes_accessed=3 << 20),
    )(table, gathered)
    diag = pl.pallas_call(
        diag_kernel,
        out_shape=jax.ShapeDtypeStruct((width, width), jnp.float32),
        in_specs=[SMEM, VMEM, VMEM],
        out_specs=VMEM,
        compiler_params=pltpu.CompilerParams(vmem_limit_bytes=4 << 20),
    )(table, parts, diag_inv[0])
    return (upper_part, lower[None], diag[None])


def solution(mesh):
    finer = Mesh(mesh.devices.reshape(8, 2, 2, 4, 2), ROW + COL)
    return jax.shard_map(
        per_device,
        mesh=finer,
        in_specs=(P(ROW, COL), P(COL, ROW, None), P(COL, None, None), P(), P(), P()),
        out_specs=(P(None, ROW, COL), P(COL, ROW, None), P(COL, None, None)),
        check_vma=False,
    )
```

```python
import functools

import jax
import jax.numpy as jnp
from jax import lax
from jax.experimental import pallas as pl
from jax.experimental.pallas import tpu as pltpu
from jax.sharding import Mesh
from jax.sharding import PartitionSpec as P

BLK = 128
SUB = 8
ROW = ("row_0", "row_1")
COL = ("col_y", "col_x", "core")
CAPS = (28,)

ROW_BLOCK, ROW_START, COL_BLOCK, COL_START = 0, 64, 72, 136
PIECE, ROW_SLOT, COL_SLOT, SOURCE, OWNER, PRESENT, AT_ROW = 144, 160, 224, 288, 352, 360, 361

SMEM = pl.BlockSpec(memory_space=pltpu.SMEM)
VMEM = pl.BlockSpec(memory_space=pltpu.VMEM)


def swapped(x, axis, bit):
    length = lax.axis_size(axis)
    return lax.ppermute(x, axis, [(i, i ^ bit) for i in range(length)])


def turned(x, axis, shift):
    length = lax.axis_size(axis)
    return lax.ppermute(x, axis, [(i, (i + shift) % length) for i in range(length)])


def member_blocks(block_lists, block_counts, block_total):
    block_ids = jnp.arange(block_total, dtype=jnp.int32)
    valid_entry = jnp.arange(block_lists.shape[1], dtype=jnp.int32)[None, :] < block_counts[:, None]
    entry_hits = (block_lists[:, :, None] == block_ids[None, None, :]) & valid_entry[:, :, None]
    return jnp.any(entry_hits, axis=1).astype(jnp.int32)


def slot_tables(listed):
    sib, blocks = listed.shape
    flat = listed.reshape(-1)
    place = jnp.arange(sib * blocks, dtype=jnp.int32)
    before = jnp.sum(jnp.where(place[None, :] < place[:, None], flat[None, :], 0), axis=1)
    here = (before[None, :] == place[:, None]) & (flat[None, :] > 0)
    code = jnp.sum(jnp.where(here, place[None, :], 0), axis=1)
    bounds = jnp.arange(sib + 1, dtype=jnp.int32) * blocks
    start = jnp.sum(jnp.where(place[None, :] < bounds[:, None], flat[None, :], 0), axis=1)
    slot = jnp.where(flat > 0, before, -1)
    return code, start, slot


def padded(values, length):
    return jnp.pad(values.astype(jnp.int32), (0, length - values.shape[0]))


def pick_kernel(cap, tab, x_ref, o_ref):
    def one(q, carry):
        o_ref[q] = x_ref[tab[SOURCE + q]]
        return carry

    lax.fori_loop(0, cap, one, 0)


def product_kernel(cap, sib, tab, g0, g1, c0, c1, ah, al, u_ref, ph_ref, pl_ref, p_ref, lhs, acc):
    parts = (g0, g1, c0, c1)
    fast = cap < sib * (ah.shape[0] // BLK)
    for i in range(4 * len(parts)):
        at = pl.multiple_of(tab[PIECE + i] * SUB, SUB) if fast else i * SUB
        p_ref[:, pl.ds(at, SUB), :] = parts[i // 4][i % 4]
    chunks, _, rows, _ = u_ref.shape

    def tile(ref, b, t):
        return ref[
            pl.ds(pl.multiple_of(b * BLK, BLK), BLK), pl.ds(pl.multiple_of(t * BLK, BLK), BLK)
        ]

    def square(ref, b0, b1, t0, t1):
        top = jnp.concatenate([tile(ref, b0, t0), tile(ref, b0, t1)], axis=1)
        low = jnp.concatenate([tile(ref, b1, t0), tile(ref, b1, t1)], axis=1)
        return jnp.concatenate([top, low], axis=0)

    def sibling(j, outer):
        r0 = tab[ROW_START + j]
        r1 = tab[ROW_START + j + 1]
        n0 = tab[COL_START + j]
        n1 = tab[COL_START + j + 1]
        quads = (r1 - r0 + 3) // 4

        def listed_panel(q):
            return jnp.where(q < r1, p_ref[jnp.minimum(q, cap - 1)], 0.0)

        def split(i, carry):
            q = r0 + 2 * i
            block = jnp.concatenate([listed_panel(q), listed_panel(q + 1)], axis=0)
            hi = block.astype(jnp.bfloat16)
            lo = (block - hi.astype(jnp.float32)).astype(jnp.bfloat16)

            @pl.when(q < r1)
            def _():
                ph_ref[q] = hi[:BLK]
                pl_ref[q] = lo[:BLK]

            @pl.when(q + 1 < r1)
            def _():
                ph_ref[q + 1] = hi[BLK:]
                pl_ref[q + 1] = lo[BLK:]

            across = hi.T
            lhs[i] = jnp.concatenate([across, across, lo.T], axis=1)
            return carry

        lax.fori_loop(0, 2 * quads, split, 0)

        def columns(o, carry):
            s = n0 + 2 * o
            t0 = tab[COL_BLOCK + s]
            t1 = tab[COL_BLOCK + s + 1]
            acc[...] = jnp.zeros_like(acc)

            def rows_of(i, inner):
                terms = []
                for k in range(2):
                    b0 = tab[ROW_BLOCK + r0 + 4 * i + 2 * k]
                    b1 = tab[ROW_BLOCK + r0 + 4 * i + 2 * k + 1]
                    hi = square(ah, b0, b1, t0, t1)
                    lo = square(al, b0, b1, t0, t1)
                    terms.append(
                        jnp.dot(
                            lhs[2 * i + k],
                            jnp.concatenate([hi, lo, hi], axis=0),
                            preferred_element_type=jnp.float32,
                        )
                    )
                acc[...] += terms[0] + terms[1]
                return inner

            lax.fori_loop(0, quads, rows_of, 0)
            for z in range(chunks):
                u_ref[z, s] = -acc[z * rows : (z + 1) * rows, :BLK]

            @pl.when(s + 1 < n1)
            def _():
                for z in range(chunks):
                    u_ref[z, s + 1] = -acc[z * rows : (z + 1) * rows, BLK:]

            return carry

        lax.fori_loop(0, (n1 - n0 + 1) // 2, columns, 0)
        return outer

    if fast:
        for j in range(sib):
            sibling(j, 0)
    else:
        lax.fori_loop(0, sib, sibling, 0)

    def clear(s, carry):
        u_ref[:, s] = jnp.zeros((chunks, rows, BLK), jnp.float32)
        return carry

    lax.fori_loop(tab[COL_START + sib], cap, clear, 0)


def unpack_kernel(tab, x_ref, o_ref):
    sib, _, cells = o_ref.shape
    blocks = cells // BLK

    def sibling(j, carry):
        for b in range(blocks):
            slot = tab[COL_SLOT + j * blocks + b]
            o_ref[j, :, b * BLK : (b + 1) * BLK] = jnp.where(
                slot >= 0, x_ref[jnp.maximum(slot, 0)], 0.0
            )
        return carry

    lax.fori_loop(0, sib, sibling, 0)


def inner_kernel(sib, tab, x_ref, hi_ref, lo_ref, o_ref):
    def sibling(j, carry):
        r0 = tab[ROW_START + j]
        r1 = tab[ROW_START + j + 1]

        def one(i, total):
            q = r0 + 2 * i
            after = jnp.where(q + 1 < r1, q + 1, q)
            x = jnp.concatenate([x_ref[q], jnp.where(after > q, x_ref[after], 0.0)], axis=1)
            x_hi = x.astype(jnp.bfloat16)
            x_lo = (x - x_hi.astype(jnp.float32)).astype(jnp.bfloat16)
            hi = jnp.concatenate([hi_ref[q], hi_ref[after]], axis=0)
            lo = jnp.concatenate([lo_ref[q], lo_ref[after]], axis=0)
            return total + jnp.dot(
                jnp.concatenate([x_hi, x_lo, x_hi], axis=1),
                jnp.concatenate([hi, hi, lo], axis=0),
                preferred_element_type=jnp.float32,
            )

        o_ref[j] = lax.fori_loop(
            0,
            (r1 - r0 + 1) // 2,
            one,
            jnp.zeros(o_ref.shape[1:], jnp.float32),
        )
        return carry

    lax.fori_loop(0, sib, sibling, 0)


def slots_kernel(sib, tab, x_ref, o_ref):
    blocks = o_ref.shape[2] // BLK

    def clear(d, carry):
        o_ref[d] = jnp.zeros(o_ref.shape[1:], jnp.float32)
        return carry

    lax.fori_loop(0, o_ref.shape[0], clear, 0)

    def sibling(j, carry):
        at = tab[OWNER + j]
        for b in range(blocks):
            slot = tab[ROW_SLOT + j * blocks + b]
            o_ref[at, :, b * BLK : (b + 1) * BLK] = jnp.where(
                slot >= 0, x_ref[jnp.maximum(slot, 0)], 0.0
            )
        return carry

    lax.fori_loop(0, sib, sibling, 0)


def place_kernel(tab, x_ref, o_ref):
    sib = x_ref.shape[0]

    def clear(d, carry):
        o_ref[d] = jnp.zeros(o_ref.shape[1:], jnp.float32)
        return carry

    lax.fori_loop(0, o_ref.shape[0], clear, 0)
    for j in range(sib):
        o_ref[tab[OWNER + j]] = x_ref[j]


def source_columns(tab, n_row):
    return [lax.rem(2 * n_row - r - tab[AT_ROW], n_row) for r in range(n_row)]


def lower_kernel(tab, x_ref, lower_ref):
    places = source_columns(tab, x_ref.shape[0])
    for b in range(lower_ref.shape[0] // BLK):
        stack = jnp.concatenate([x_ref[p, :, b * BLK : (b + 1) * BLK] for p in places], axis=0)
        lower_ref[b * BLK : (b + 1) * BLK, :] = stack.T


def diag_kernel(tab, x_ref, diag_ref, out_ref):
    total = jnp.concatenate([x_ref[p] for p in source_columns(tab, x_ref.shape[0])], axis=0)
    out_ref[...] = jnp.where(tab[PRESENT] > 0, diag_ref[...] - total, 0.0)


def ring_term(u, z, first, last, lead):
    part = lax.dynamic_index_in_dim(u, (z + 2 * u.shape[0]) % u.shape[0], 0, keepdims=False)
    part = part[first:last]
    return part if lead == 1 else part.reshape(lead, -1, *part.shape[1:])


def halves(parts, half, rows):
    return jnp.concatenate([lax.dynamic_slice_in_dim(x, half * rows, rows, 1) for x in parts])


def listed_products(cap, sib, table, scattered, a_hi, a_lo):
    row_cells, col_cells = a_hi.shape
    pieces, blocks, sub, width = scattered.shape
    near_chunks = lax.axis_size("row_0")
    half_rows = width // (near_chunks * lax.axis_size("row_1"))
    own = pl.pallas_call(
        functools.partial(pick_kernel, cap),
        out_shape=jax.ShapeDtypeStruct((cap, sub, width), jnp.float32),
        in_specs=[SMEM, VMEM],
        out_specs=VMEM,
        compiler_params=pltpu.CompilerParams(vmem_limit_bytes=8 << 20),
    )(table, scattered.reshape(pieces * blocks, sub, width))
    if cap < sib * blocks:
        right = turned(own, "col_x", 1)
        left = turned(own, "col_x", -1)
        beside = swapped(own, "col_y", 1)
        right_beside = turned(beside, "col_x", 1)
        left_beside = turned(beside, "col_x", -1)
        right_two = turned(right, "col_x", 1)
        left_two = turned(left_beside, "col_x", -1)
        g0 = jnp.stack([own, beside, right, left])
        g1 = jnp.stack([right_beside, left_beside, right_two, left_two])
        c0 = swapped(g0, "core", 1)
        c1 = swapped(g1, "core", 1)
    else:
        all_pieces = lax.all_to_all(
            jnp.broadcast_to(own[None], (pieces, *own.shape)), COL, 0, 0, tiled=True
        )
        g0, g1, c0, c1 = (all_pieces[i : i + 4] for i in range(0, pieces, 4))
    chunk = width // near_chunks
    u, p_hi, p_lo = pl.pallas_call(
        functools.partial(product_kernel, cap, sib),
        out_shape=(
            jax.ShapeDtypeStruct((near_chunks, cap, chunk, BLK), jnp.float32),
            jax.ShapeDtypeStruct((cap, BLK, width), jnp.bfloat16),
            jax.ShapeDtypeStruct((cap, BLK, width), jnp.bfloat16),
        ),
        in_specs=[SMEM] + [VMEM] * 6,
        out_specs=(VMEM, VMEM, VMEM),
        scratch_shapes=[
            pltpu.VMEM((cap, BLK, width), jnp.float32),
            pltpu.VMEM((row_cells // BLK // 2 + 1, width, 6 * BLK), jnp.bfloat16),
            pltpu.VMEM((width, 2 * BLK), jnp.float32),
        ],
        compiler_params=pltpu.CompilerParams(vmem_limit_bytes=(26 if cap < sib * blocks else 34) << 20),
    )(table, g0, g1, c0, c1, a_hi, a_lo)
    z = lax.axis_index("row_0")
    if cap < sib * blocks:
        strands = [(0, cap // 2, 1, 1), (cap // 2, cap, 2, -1)]
        near = [ring_term(u, z - way, first, last, lead) for first, last, lead, way in strands]
        for step in range(1, near_chunks):
            near = [
                turned(x, "row_0", way) + ring_term(u, z - way * (1 + step), first, last, lead)
                for x, (first, last, lead, way) in zip(near, strands)
            ]
        near = [x.reshape(-1, *x.shape[-2:]) for x in near]
    else:
        near = [jnp.sum(lax.all_to_all(u, "row_0", 0, 0, tiled=True), axis=0)]
    half = lax.axis_index("row_1")
    sent = halves(near, 1 - half, half_rows)
    kept = halves(near, half, half_rows)
    n_row = lax.axis_size(ROW)
    n_col = lax.axis_size(COL)
    spots = [(r, c) for r in range(n_row) for c in range(n_col)]
    across = [(r * n_col + c, r * n_col + (-r - c) % n_col) for r, c in spots]
    over = [(r * n_col + c, (r ^ 1) * n_col + (-(r ^ 1) - c) % n_col) for r, c in spots]
    along = [(r * n_col + k, (-r - k) % n_row * n_col + k) for r, k in spots]
    midway = lax.ppermute(kept, ROW + COL, across) + lax.ppermute(sent, ROW + COL, over)
    moved = lax.ppermute(midway, ROW + COL, along)
    sent, moved = lax.optimization_barrier((sent, moved))
    total = kept + swapped(sent, "row_1", 1)
    upper_part = pl.pallas_call(
        unpack_kernel,
        out_shape=jax.ShapeDtypeStruct((sib, half_rows, col_cells), jnp.float32),
        in_specs=[SMEM, VMEM],
        out_specs=VMEM,
        compiler_params=pltpu.CompilerParams(vmem_limit_bytes=8 << 20),
        cost_estimate=pl.CostEstimate(flops=0, transcendentals=0, bytes_accessed=1 << 20),
    )(table, total)
    slots = pl.pallas_call(
        functools.partial(slots_kernel, sib),
        out_shape=jax.ShapeDtypeStruct((n_col, half_rows, row_cells), jnp.float32),
        in_specs=[SMEM, VMEM],
        out_specs=VMEM,
        compiler_params=pltpu.CompilerParams(vmem_limit_bytes=8 << 20),
        cost_estimate=pl.CostEstimate(flops=0, transcendentals=0, bytes_accessed=2 << 20),
    )(table, moved)
    inner = pl.pallas_call(
        functools.partial(inner_kernel, sib),
        out_shape=jax.ShapeDtypeStruct((sib, half_rows, width), jnp.float32),
        in_specs=[SMEM] + [VMEM] * 3,
        out_specs=VMEM,
        compiler_params=pltpu.CompilerParams(vmem_limit_bytes=12 << 20),
        cost_estimate=pl.CostEstimate(
            flops=6 * cap * half_rows * BLK * width, transcendentals=0, bytes_accessed=6 << 20
        ),
    )(table, moved, p_hi, p_lo)
    return upper_part, slots, inner


def piece_columns():
    y = lax.axis_index("col_y")
    x = lax.axis_index("col_x")
    core = lax.axis_index("core")
    n_x = lax.axis_size("col_x")
    places = [(y, x), (1 - y, x), (y, x - 1), (y, x + 1)]
    places += [(1 - y, x - 1), (1 - y, x + 1), (y, x - 2), (1 - y, x + 2)]
    return jnp.stack(
        [
            (py * n_x + (px + n_x) % n_x) * 2 + pc
            for pc in (core, 1 - core)
            for py, px in places
        ]
    ).astype(jnp.int32)


def per_device(anc_inverse, l_store, diag_inv, block_lists, block_counts, sibling_columns):
    row_cells, col_cells = anc_inverse.shape
    width = l_store.shape[2]
    sib = sibling_columns.shape[0]
    n_col = lax.axis_size(COL)
    n_row = lax.axis_size(ROW)
    row_index = lax.axis_index(ROW)
    col_index = lax.axis_index(COL)
    blocks = row_cells // BLK
    cut = l_store[0].reshape(blocks, n_col, SUB, width).transpose(1, 0, 2, 3)
    scattered = lax.all_to_all(cut, COL, 0, 0, tiled=True)
    rounded = lax.reduce_precision(anc_inverse, 8, 7)
    a_hi = rounded.astype(jnp.bfloat16)
    a_lo = (anc_inverse - rounded).astype(jnp.bfloat16)

    listed = member_blocks(block_lists, block_counts, n_row * blocks)
    groups = listed.reshape(sib, n_row, blocks)
    most = jnp.max(jnp.sum(groups, axis=(0, 2)))
    row_code, row_start, row_slot = slot_tables(
        lax.dynamic_index_in_dim(groups, row_index, 1, keepdims=False)
    )
    col_code, col_start, col_slot = slot_tables(
        lax.dynamic_index_in_dim(groups, col_index, 1, keepdims=False)
    )
    owner = jnp.sum(
        jnp.where(
            (row_code // blocks)[:, None] == jnp.arange(sib, dtype=jnp.int32)[None, :],
            sibling_columns[None, :],
            0,
        ),
        axis=1,
    )
    table = jnp.concatenate(
        [
            padded(row_code % blocks, 64),
            padded(row_start, 8),
            padded(col_code % blocks, 64),
            padded(col_start, 8),
            padded(piece_columns(), 16),
            padded(row_slot, 64),
            padded(col_slot, 64),
            padded(owner * blocks + row_code % blocks, 64),
            padded(sibling_columns, 8),
            jnp.stack([jnp.any(sibling_columns == col_index).astype(jnp.int32), row_index]),
        ]
    )
    caps = [c for c in CAPS if c < sib * blocks] + [sib * blocks]
    which = sum((most > c).astype(jnp.int32) for c in caps[:-1])
    upper_part, slots, inner = lax.switch(
        which,
        [functools.partial(listed_products, c, sib) for c in caps],
        table,
        scattered,
        a_hi,
        a_lo,
    )
    place = lambda x: pl.pallas_call(
        place_kernel,
        out_shape=jax.ShapeDtypeStruct((n_col, *x.shape[1:]), jnp.float32),
        in_specs=[SMEM, VMEM],
        out_specs=VMEM,
        compiler_params=pltpu.CompilerParams(vmem_limit_bytes=8 << 20),
    )(table, x)
    gathered = lax.all_to_all(slots, COL, 0, 0, tiled=True)
    for bit in (1, 4):
        others = []
        for away in (bit, 2 * bit, 3 * bit):
            pairs = [
                (r * n_col + k, (r ^ away) * n_col + (k + r - (r ^ away)) % n_col)
                for r in range(n_row)
                for k in range(n_col)
            ]
            others.append(lax.ppermute(inner, ROW + COL, pairs))
        inner = (inner + others[0]) + (others[1] + others[2])
    gathered, inner = lax.optimization_barrier((gathered, inner))
    parts = lax.all_to_all(place(inner), COL, 0, 0, tiled=True)
    lower = pl.pallas_call(
        lower_kernel,
        out_shape=jax.ShapeDtypeStruct((row_cells, width), jnp.float32),
        in_specs=[SMEM, VMEM],
        out_specs=VMEM,
        compiler_params=pltpu.CompilerParams(vmem_limit_bytes=8 << 20),
        cost_estimate=pl.CostEstimate(flops=0, transcendentals=0, bytes_accessed=3 << 20),
    )(table, gathered)
    diag = pl.pallas_call(
        diag_kernel,
        out_shape=jax.ShapeDtypeStruct((width, width), jnp.float32),
        in_specs=[SMEM, VMEM, VMEM],
        out_specs=VMEM,
        compiler_params=pltpu.CompilerParams(vmem_limit_bytes=4 << 20),
    )(table, parts, diag_inv[0])
    return (upper_part, lower[None], diag[None])


def solution(mesh):
    finer = Mesh(mesh.devices.reshape(8, 2, 2, 4, 2), ROW + COL)
    return jax.shard_map(
        per_device,
        mesh=finer,
        in_specs=(P(ROW, COL), P(COL, ROW, None), P(COL, None, None), P(), P(), P()),
        out_specs=(P(None, ROW, COL), P(COL, ROW, None), P(COL, None, None)),
        check_vma=False,
    )
```

```python
import functools

import jax
import jax.numpy as jnp
from jax import lax
from jax.experimental import pallas as pl
from jax.experimental.pallas import tpu as pltpu
from jax.sharding import Mesh
from jax.sharding import PartitionSpec as P

BLK = 128
SUB = 8
ROW = ("row_0", "row_1")
COL = ("col_y", "col_x", "core")
CAPS = (28,)

ROW_BLOCK, ROW_START, COL_BLOCK, COL_START = 0, 64, 72, 136
PIECE, ROW_SLOT, COL_SLOT, SOURCE, OWNER, PRESENT, AT_ROW = 144, 160, 224, 288, 352, 360, 361

SMEM = pl.BlockSpec(memory_space=pltpu.SMEM)
VMEM = pl.BlockSpec(memory_space=pltpu.VMEM)


def swapped(x, axis, bit):
    length = lax.axis_size(axis)
    return lax.ppermute(x, axis, [(i, i ^ bit) for i in range(length)])


def turned(x, axis, shift):
    length = lax.axis_size(axis)
    return lax.ppermute(x, axis, [(i, (i + shift) % length) for i in range(length)])


def member_blocks(block_lists, block_counts, block_total):
    block_ids = jnp.arange(block_total, dtype=jnp.int32)
    valid_entry = jnp.arange(block_lists.shape[1], dtype=jnp.int32)[None, :] < block_counts[:, None]
    entry_hits = (block_lists[:, :, None] == block_ids[None, None, :]) & valid_entry[:, :, None]
    return jnp.any(entry_hits, axis=1).astype(jnp.int32)


def slot_tables(listed):
    sib, blocks = listed.shape
    flat = listed.reshape(-1)
    place = jnp.arange(sib * blocks, dtype=jnp.int32)
    before = jnp.sum(jnp.where(place[None, :] < place[:, None], flat[None, :], 0), axis=1)
    here = (before[None, :] == place[:, None]) & (flat[None, :] > 0)
    code = jnp.sum(jnp.where(here, place[None, :], 0), axis=1)
    bounds = jnp.arange(sib + 1, dtype=jnp.int32) * blocks
    start = jnp.sum(jnp.where(place[None, :] < bounds[:, None], flat[None, :], 0), axis=1)
    slot = jnp.where(flat > 0, before, -1)
    return code, start, slot


def padded(values, length):
    return jnp.pad(values.astype(jnp.int32), (0, length - values.shape[0]))


def cut_kernel(x_ref, o_ref):
    pieces, blocks, rows, _ = o_ref.shape

    def block(b, carry):
        for p in range(pieces):
            at = pl.multiple_of((b * pieces + p) * rows, SUB)
            o_ref[p, b] = x_ref[pl.ds(at, rows), :]
        return carry

    lax.fori_loop(0, blocks, block, 0)


def pick_kernel(cap, tab, x_ref, o_ref):
    def one(q, carry):
        o_ref[q] = x_ref[tab[SOURCE + q]]
        return carry

    lax.fori_loop(0, cap, one, 0)


def product_kernel(cap, sib, tab, g0, g1, c0, c1, ah, al, u_ref, ph_ref, pl_ref, p_ref, lhs, acc):
    parts = (g0, g1, c0, c1)
    fast = cap < sib * (ah.shape[0] // BLK)
    for i in range(4 * len(parts)):
        at = pl.multiple_of(tab[PIECE + i] * SUB, SUB) if fast else i * SUB
        p_ref[:, pl.ds(at, SUB), :] = parts[i // 4][i % 4]
    chunks, _, rows, _ = u_ref.shape

    def tile(ref, b, t):
        return ref[
            pl.ds(pl.multiple_of(b * BLK, BLK), BLK), pl.ds(pl.multiple_of(t * BLK, BLK), BLK)
        ]

    def square(ref, b0, b1, t0, t1):
        top = jnp.concatenate([tile(ref, b0, t0), tile(ref, b0, t1)], axis=1)
        low = jnp.concatenate([tile(ref, b1, t0), tile(ref, b1, t1)], axis=1)
        return jnp.concatenate([top, low], axis=0)

    def sibling(j, outer):
        r0 = tab[ROW_START + j]
        r1 = tab[ROW_START + j + 1]
        n0 = tab[COL_START + j]
        n1 = tab[COL_START + j + 1]
        quads = (r1 - r0 + 3) // 4

        def listed_panel(q):
            return jnp.where(q < r1, p_ref[jnp.minimum(q, cap - 1)], 0.0)

        def split(i, carry):
            q = r0 + 2 * i
            block = jnp.concatenate([listed_panel(q), listed_panel(q + 1)], axis=0)
            hi = block.astype(jnp.bfloat16)
            lo = (block - hi.astype(jnp.float32)).astype(jnp.bfloat16)

            @pl.when(q < r1)
            def _():
                ph_ref[q] = hi[:BLK]
                pl_ref[q] = lo[:BLK]

            @pl.when(q + 1 < r1)
            def _():
                ph_ref[q + 1] = hi[BLK:]
                pl_ref[q + 1] = lo[BLK:]

            across = hi.T
            lhs[i] = jnp.concatenate([across, across, lo.T], axis=1)
            return carry

        lax.fori_loop(0, 2 * quads, split, 0)

        def columns(o, carry):
            s = n0 + 2 * o
            t0 = tab[COL_BLOCK + s]
            t1 = tab[COL_BLOCK + s + 1]
            acc[...] = jnp.zeros_like(acc)

            def rows_of(i, inner):
                terms = []
                for k in range(2):
                    b0 = tab[ROW_BLOCK + r0 + 4 * i + 2 * k]
                    b1 = tab[ROW_BLOCK + r0 + 4 * i + 2 * k + 1]
                    hi = square(ah, b0, b1, t0, t1)
                    lo = square(al, b0, b1, t0, t1)
                    terms.append(
                        jnp.dot(
                            lhs[2 * i + k],
                            jnp.concatenate([hi, lo, hi], axis=0),
                            preferred_element_type=jnp.float32,
                        )
                    )
                acc[...] += terms[0] + terms[1]
                return inner

            lax.fori_loop(0, quads, rows_of, 0)
            for z in range(chunks):
                u_ref[z, s] = -acc[z * rows : (z + 1) * rows, :BLK]

            @pl.when(s + 1 < n1)
            def _():
                for z in range(chunks):
                    u_ref[z, s + 1] = -acc[z * rows : (z + 1) * rows, BLK:]

            return carry

        lax.fori_loop(0, (n1 - n0 + 1) // 2, columns, 0)
        return outer

    if fast:
        for j in range(sib):
            sibling(j, 0)
    else:
        lax.fori_loop(0, sib, sibling, 0)

    def clear(s, carry):
        u_ref[:, s] = jnp.zeros((chunks, rows, BLK), jnp.float32)
        return carry

    lax.fori_loop(tab[COL_START + sib], cap, clear, 0)


def unpack_kernel(tab, x_ref, o_ref):
    sib, _, cells = o_ref.shape
    blocks = cells // BLK

    def sibling(j, carry):
        for b in range(blocks):
            slot = tab[COL_SLOT + j * blocks + b]
            o_ref[j, :, b * BLK : (b + 1) * BLK] = jnp.where(
                slot >= 0, x_ref[jnp.maximum(slot, 0)], 0.0
            )
        return carry

    lax.fori_loop(0, sib, sibling, 0)


def inner_kernel(sib, tab, x_ref, hi_ref, lo_ref, o_ref):
    def sibling(j, carry):
        r0 = tab[ROW_START + j]
        r1 = tab[ROW_START + j + 1]

        def one(i, total):
            q = r0 + 2 * i
            after = jnp.where(q + 1 < r1, q + 1, q)
            x = jnp.concatenate([x_ref[q], jnp.where(after > q, x_ref[after], 0.0)], axis=1)
            x_hi = x.astype(jnp.bfloat16)
            x_lo = (x - x_hi.astype(jnp.float32)).astype(jnp.bfloat16)
            hi = jnp.concatenate([hi_ref[q], hi_ref[after]], axis=0)
            lo = jnp.concatenate([lo_ref[q], lo_ref[after]], axis=0)
            return total + jnp.dot(
                jnp.concatenate([x_hi, x_lo, x_hi], axis=1),
                jnp.concatenate([hi, hi, lo], axis=0),
                preferred_element_type=jnp.float32,
            )

        o_ref[j] = lax.fori_loop(
            0,
            (r1 - r0 + 1) // 2,
            one,
            jnp.zeros(o_ref.shape[1:], jnp.float32),
        )
        return carry

    lax.fori_loop(0, sib, sibling, 0)


def slots_kernel(sib, tab, x_ref, o_ref):
    blocks = o_ref.shape[2] // BLK

    def clear(d, carry):
        o_ref[d] = jnp.zeros(o_ref.shape[1:], jnp.float32)
        return carry

    lax.fori_loop(0, o_ref.shape[0], clear, 0)

    def sibling(j, carry):
        at = tab[OWNER + j]
        for b in range(blocks):
            slot = tab[ROW_SLOT + j * blocks + b]
            o_ref[at, :, b * BLK : (b + 1) * BLK] = jnp.where(
                slot >= 0, x_ref[jnp.maximum(slot, 0)], 0.0
            )
        return carry

    lax.fori_loop(0, sib, sibling, 0)


def place_kernel(tab, x_ref, o_ref):
    sib = x_ref.shape[0]

    def clear(d, carry):
        o_ref[d] = jnp.zeros(o_ref.shape[1:], jnp.float32)
        return carry

    lax.fori_loop(0, o_ref.shape[0], clear, 0)
    for j in range(sib):
        o_ref[tab[OWNER + j]] = x_ref[j]


def source_columns(tab, n_row):
    return [lax.rem(2 * n_row - r - tab[AT_ROW], n_row) for r in range(n_row)]


def lower_kernel(tab, x_ref, lower_ref):
    places = source_columns(tab, x_ref.shape[0])
    for b in range(lower_ref.shape[0] // BLK):
        stack = jnp.concatenate([x_ref[p, :, b * BLK : (b + 1) * BLK] for p in places], axis=0)
        lower_ref[b * BLK : (b + 1) * BLK, :] = stack.T


def diag_kernel(tab, x_ref, diag_ref, out_ref):
    total = jnp.concatenate([x_ref[p] for p in source_columns(tab, x_ref.shape[0])], axis=0)
    out_ref[...] = jnp.where(tab[PRESENT] > 0, diag_ref[...] - total, 0.0)


def ring_term(u, z, first, last, lead):
    part = lax.dynamic_index_in_dim(u, (z + 2 * u.shape[0]) % u.shape[0], 0, keepdims=False)
    part = part[first:last]
    return part if lead == 1 else part.reshape(lead, -1, *part.shape[1:])


def halves(parts, half, rows):
    return jnp.concatenate([lax.dynamic_slice_in_dim(x, half * rows, rows, 1) for x in parts])


def listed_products(cap, sib, table, scattered, a_hi, a_lo):
    row_cells, col_cells = a_hi.shape
    pieces, blocks, sub, width = scattered.shape
    near_chunks = lax.axis_size("row_0")
    half_rows = width // (near_chunks * lax.axis_size("row_1"))
    own = pl.pallas_call(
        functools.partial(pick_kernel, cap),
        out_shape=jax.ShapeDtypeStruct((cap, sub, width), jnp.float32),
        in_specs=[SMEM, VMEM],
        out_specs=VMEM,
        compiler_params=pltpu.CompilerParams(vmem_limit_bytes=8 << 20),
    )(table, scattered.reshape(pieces * blocks, sub, width))
    if cap < sib * blocks:
        right = turned(own, "col_x", 1)
        left = turned(own, "col_x", -1)
        beside = swapped(own, "col_y", 1)
        right_beside = turned(beside, "col_x", 1)
        left_beside = turned(beside, "col_x", -1)
        right_two = turned(right, "col_x", 1)
        left_two = turned(left_beside, "col_x", -1)
        g0 = jnp.stack([own, beside, right, left])
        g1 = jnp.stack([right_beside, left_beside, right_two, left_two])
        c0 = swapped(g0, "core", 1)
        c1 = swapped(g1, "core", 1)
    else:
        all_pieces = lax.all_to_all(
            jnp.broadcast_to(own[None], (pieces, *own.shape)), COL, 0, 0, tiled=True
        )
        g0, g1, c0, c1 = (all_pieces[i : i + 4] for i in range(0, pieces, 4))
    chunk = width // near_chunks
    u, p_hi, p_lo = pl.pallas_call(
        functools.partial(product_kernel, cap, sib),
        out_shape=(
            jax.ShapeDtypeStruct((near_chunks, cap, chunk, BLK), jnp.float32),
            jax.ShapeDtypeStruct((cap, BLK, width), jnp.bfloat16),
            jax.ShapeDtypeStruct((cap, BLK, width), jnp.bfloat16),
        ),
        in_specs=[SMEM] + [VMEM] * 6,
        out_specs=(VMEM, VMEM, VMEM),
        scratch_shapes=[
            pltpu.VMEM((cap, BLK, width), jnp.float32),
            pltpu.VMEM((row_cells // BLK // 2 + 1, width, 6 * BLK), jnp.bfloat16),
            pltpu.VMEM((width, 2 * BLK), jnp.float32),
        ],
        compiler_params=pltpu.CompilerParams(vmem_limit_bytes=(26 if cap < sib * blocks else 34) << 20),
    )(table, g0, g1, c0, c1, a_hi, a_lo)
    z = lax.axis_index("row_0")
    if cap < sib * blocks:
        strands = [(0, cap // 2, 1, 1), (cap // 2, cap, 2, -1)]
        near = [ring_term(u, z - way, first, last, lead) for first, last, lead, way in strands]
        for step in range(1, near_chunks):
            near = [
                turned(x, "row_0", way) + ring_term(u, z - way * (1 + step), first, last, lead)
                for x, (first, last, lead, way) in zip(near, strands)
            ]
        near = [x.reshape(-1, *x.shape[-2:]) for x in near]
    else:
        near = [jnp.sum(lax.all_to_all(u, "row_0", 0, 0, tiled=True), axis=0)]
    half = lax.axis_index("row_1")
    sent = halves(near, 1 - half, half_rows)
    kept = halves(near, half, half_rows)
    n_row = lax.axis_size(ROW)
    n_col = lax.axis_size(COL)
    spots = [(r, c) for r in range(n_row) for c in range(n_col)]
    across = [(r * n_col + c, r * n_col + (-r - c) % n_col) for r, c in spots]
    over = [(r * n_col + c, (r ^ 1) * n_col + (-(r ^ 1) - c) % n_col) for r, c in spots]
    along = [(r * n_col + k, (-r - k) % n_row * n_col + k) for r, k in spots]
    midway = lax.ppermute(kept, ROW + COL, across) + lax.ppermute(sent, ROW + COL, over)
    moved = lax.ppermute(midway, ROW + COL, along)
    sent, moved = lax.optimization_barrier((sent, moved))
    total = kept + swapped(sent, "row_1", 1)
    upper_part = pl.pallas_call(
        unpack_kernel,
        out_shape=jax.ShapeDtypeStruct((sib, half_rows, col_cells), jnp.float32),
        in_specs=[SMEM, VMEM],
        out_specs=VMEM,
        compiler_params=pltpu.CompilerParams(vmem_limit_bytes=8 << 20),
        cost_estimate=pl.CostEstimate(flops=0, transcendentals=0, bytes_accessed=1 << 20),
    )(table, total)
    slots = pl.pallas_call(
        functools.partial(slots_kernel, sib),
        out_shape=jax.ShapeDtypeStruct((n_col, half_rows, row_cells), jnp.float32),
        in_specs=[SMEM, VMEM],
        out_specs=VMEM,
        compiler_params=pltpu.CompilerParams(vmem_limit_bytes=8 << 20),
        cost_estimate=pl.CostEstimate(flops=0, transcendentals=0, bytes_accessed=2 << 20),
    )(table, moved)
    inner = pl.pallas_call(
        functools.partial(inner_kernel, sib),
        out_shape=jax.ShapeDtypeStruct((sib, half_rows, width), jnp.float32),
        in_specs=[SMEM] + [VMEM] * 3,
        out_specs=VMEM,
        compiler_params=pltpu.CompilerParams(vmem_limit_bytes=12 << 20),
        cost_estimate=pl.CostEstimate(
            flops=6 * cap * half_rows * BLK * width, transcendentals=0, bytes_accessed=6 << 20
        ),
    )(table, moved, p_hi, p_lo)
    return upper_part, slots, inner


def piece_columns():
    y = lax.axis_index("col_y")
    x = lax.axis_index("col_x")
    core = lax.axis_index("core")
    n_x = lax.axis_size("col_x")
    places = [(y, x), (1 - y, x), (y, x - 1), (y, x + 1)]
    places += [(1 - y, x - 1), (1 - y, x + 1), (y, x - 2), (1 - y, x + 2)]
    return jnp.stack(
        [
            (py * n_x + (px + n_x) % n_x) * 2 + pc
            for pc in (core, 1 - core)
            for py, px in places
        ]
    ).astype(jnp.int32)


def per_device(anc_inverse, l_store, diag_inv, block_lists, block_counts, sibling_columns):
    row_cells, col_cells = anc_inverse.shape
    width = l_store.shape[2]
    sib = sibling_columns.shape[0]
    n_col = lax.axis_size(COL)
    n_row = lax.axis_size(ROW)
    row_index = lax.axis_index(ROW)
    col_index = lax.axis_index(COL)
    blocks = row_cells // BLK
    cut = pl.pallas_call(
        cut_kernel,
        out_shape=jax.ShapeDtypeStruct((n_col, blocks, SUB, width), jnp.float32),
        in_specs=[VMEM],
        out_specs=VMEM,
        compiler_params=pltpu.CompilerParams(vmem_limit_bytes=4 << 20),
    )(l_store[0])
    scattered = lax.all_to_all(cut, COL, 0, 0, tiled=True)
    rounded = lax.reduce_precision(anc_inverse, 8, 7)
    a_hi = rounded.astype(jnp.bfloat16)
    a_lo = (anc_inverse - rounded).astype(jnp.bfloat16)

    listed = member_blocks(block_lists, block_counts, n_row * blocks)
    groups = listed.reshape(sib, n_row, blocks)
    most = jnp.max(jnp.sum(groups, axis=(0, 2)))
    row_code, row_start, row_slot = slot_tables(
        lax.dynamic_index_in_dim(groups, row_index, 1, keepdims=False)
    )
    col_code, col_start, col_slot = slot_tables(
        lax.dynamic_index_in_dim(groups, col_index, 1, keepdims=False)
    )
    owner = jnp.sum(
        jnp.where(
            (row_code // blocks)[:, None] == jnp.arange(sib, dtype=jnp.int32)[None, :],
            sibling_columns[None, :],
            0,
        ),
        axis=1,
    )
    table = jnp.concatenate(
        [
            padded(row_code % blocks, 64),
            padded(row_start, 8),
            padded(col_code % blocks, 64),
            padded(col_start, 8),
            padded(piece_columns(), 16),
            padded(row_slot, 64),
            padded(col_slot, 64),
            padded(owner * blocks + row_code % blocks, 64),
            padded(sibling_columns, 8),
            jnp.stack([jnp.any(sibling_columns == col_index).astype(jnp.int32), row_index]),
        ]
    )
    caps = [c for c in CAPS if c < sib * blocks] + [sib * blocks]
    which = sum((most > c).astype(jnp.int32) for c in caps[:-1])
    upper_part, slots, inner = lax.switch(
        which,
        [functools.partial(listed_products, c, sib) for c in caps],
        table,
        scattered,
        a_hi,
        a_lo,
    )
    place = lambda x: pl.pallas_call(
        place_kernel,
        out_shape=jax.ShapeDtypeStruct((n_col, *x.shape[1:]), jnp.float32),
        in_specs=[SMEM, VMEM],
        out_specs=VMEM,
        compiler_params=pltpu.CompilerParams(vmem_limit_bytes=8 << 20),
    )(table, x)
    gathered = lax.all_to_all(slots, COL, 0, 0, tiled=True)
    for bit in (1, 4):
        others = []
        for away in (bit, 2 * bit, 3 * bit):
            pairs = [
                (r * n_col + k, (r ^ away) * n_col + (k + r - (r ^ away)) % n_col)
                for r in range(n_row)
                for k in range(n_col)
            ]
            others.append(lax.ppermute(inner, ROW + COL, pairs))
        inner = (inner + others[0]) + (others[1] + others[2])
    gathered, inner = lax.optimization_barrier((gathered, inner))
    parts = lax.all_to_all(place(inner), COL, 0, 0, tiled=True)
    lower = pl.pallas_call(
        lower_kernel,
        out_shape=jax.ShapeDtypeStruct((row_cells, width), jnp.float32),
        in_specs=[SMEM, VMEM],
        out_specs=VMEM,
        compiler_params=pltpu.CompilerParams(vmem_limit_bytes=8 << 20),
        cost_estimate=pl.CostEstimate(flops=0, transcendentals=0, bytes_accessed=3 << 20),
    )(table, gathered)
    diag = pl.pallas_call(
        diag_kernel,
        out_shape=jax.ShapeDtypeStruct((width, width), jnp.float32),
        in_specs=[SMEM, VMEM, VMEM],
        out_specs=VMEM,
        compiler_params=pltpu.CompilerParams(vmem_limit_bytes=4 << 20),
    )(table, parts, diag_inv[0])
    return (upper_part, lower[None], diag[None])


def solution(mesh):
    finer = Mesh(mesh.devices.reshape(8, 2, 2, 4, 2), ROW + COL)
    return jax.shard_map(
        per_device,
        mesh=finer,
        in_specs=(P(ROW, COL), P(COL, ROW, None), P(COL, None, None), P(), P(), P()),
        out_specs=(P(None, ROW, COL), P(COL, ROW, None), P(COL, None, None)),
        check_vma=False,
    )
```

```python
import functools

import jax
import jax.numpy as jnp
from jax import lax
from jax.experimental import pallas as pl
from jax.experimental.pallas import tpu as pltpu
from jax.sharding import Mesh
from jax.sharding import PartitionSpec as P

BLK = 128
SUB = 8
ROW = ("row_0", "row_1")
COL = ("col_y", "col_x", "core")
CAPS = (30,)

ROW_BLOCK, ROW_START, COL_BLOCK, COL_START = 0, 64, 72, 136
PIECE, ROW_SLOT, COL_SLOT, SOURCE, OWNER, PRESENT, AT_ROW = 144, 160, 224, 288, 352, 360, 361

SMEM = pl.BlockSpec(memory_space=pltpu.SMEM)
VMEM = pl.BlockSpec(memory_space=pltpu.VMEM)


def swapped(x, axis, bit):
    length = lax.axis_size(axis)
    return lax.ppermute(x, axis, [(i, i ^ bit) for i in range(length)])


def turned(x, axis, shift):
    length = lax.axis_size(axis)
    return lax.ppermute(x, axis, [(i, (i + shift) % length) for i in range(length)])


def member_blocks(block_lists, block_counts, block_total):
    block_ids = jnp.arange(block_total, dtype=jnp.int32)
    valid_entry = jnp.arange(block_lists.shape[1], dtype=jnp.int32)[None, :] < block_counts[:, None]
    entry_hits = (block_lists[:, :, None] == block_ids[None, None, :]) & valid_entry[:, :, None]
    return jnp.any(entry_hits, axis=1).astype(jnp.int32)


def slot_tables(listed):
    sib, blocks = listed.shape
    flat = listed.reshape(-1)
    place = jnp.arange(sib * blocks, dtype=jnp.int32)
    before = jnp.sum(jnp.where(place[None, :] < place[:, None], flat[None, :], 0), axis=1)
    here = (before[None, :] == place[:, None]) & (flat[None, :] > 0)
    code = jnp.sum(jnp.where(here, place[None, :], 0), axis=1)
    bounds = jnp.arange(sib + 1, dtype=jnp.int32) * blocks
    start = jnp.sum(jnp.where(place[None, :] < bounds[:, None], flat[None, :], 0), axis=1)
    slot = jnp.where(flat > 0, before, -1)
    return code, start, slot


def padded(values, length):
    return jnp.pad(values.astype(jnp.int32), (0, length - values.shape[0]))


def pick_kernel(cap, tab, x_ref, o_ref):
    def one(q, carry):
        o_ref[q] = x_ref[tab[SOURCE + q]]
        return carry

    lax.fori_loop(0, cap, one, 0)


def product_kernel(cap, sib, tab, g0, g1, c0, c1, ah, al, u_ref, ph_ref, pl_ref, p_ref, lhs, acc):
    parts = (g0, g1, c0, c1)
    fast = cap < sib * (ah.shape[0] // BLK)
    for i in range(4 * len(parts)):
        at = pl.multiple_of(tab[PIECE + i] * SUB, SUB) if fast else i * SUB
        p_ref[:, pl.ds(at, SUB), :] = parts[i // 4][i % 4]
    chunks, _, rows, _ = u_ref.shape

    def tile(ref, b, t):
        return ref[
            pl.ds(pl.multiple_of(b * BLK, BLK), BLK), pl.ds(pl.multiple_of(t * BLK, BLK), BLK)
        ]

    def square(ref, b0, b1, t0, t1):
        top = jnp.concatenate([tile(ref, b0, t0), tile(ref, b0, t1)], axis=1)
        low = jnp.concatenate([tile(ref, b1, t0), tile(ref, b1, t1)], axis=1)
        return jnp.concatenate([top, low], axis=0)

    def sibling(j, outer):
        r0 = tab[ROW_START + j]
        r1 = tab[ROW_START + j + 1]
        n0 = tab[COL_START + j]
        n1 = tab[COL_START + j + 1]
        quads = (r1 - r0 + 3) // 4

        def listed_panel(q):
            return jnp.where(q < r1, p_ref[jnp.minimum(q, cap - 1)], 0.0)

        def split(i, carry):
            q = r0 + 2 * i
            block = jnp.concatenate([listed_panel(q), listed_panel(q + 1)], axis=0)
            hi = block.astype(jnp.bfloat16)
            lo = (block - hi.astype(jnp.float32)).astype(jnp.bfloat16)

            @pl.when(q < r1)
            def _():
                ph_ref[q] = hi[:BLK]
                pl_ref[q] = lo[:BLK]

            @pl.when(q + 1 < r1)
            def _():
                ph_ref[q + 1] = hi[BLK:]
                pl_ref[q + 1] = lo[BLK:]

            across = hi.T
            lhs[i] = jnp.concatenate([across, across, lo.T], axis=1)
            return carry

        lax.fori_loop(0, 2 * quads, split, 0)

        def columns(o, carry):
            s = n0 + 2 * o
            t0 = tab[COL_BLOCK + s]
            t1 = tab[COL_BLOCK + s + 1]
            acc[...] = jnp.zeros_like(acc)

            def rows_of(i, inner):
                terms = []
                for k in range(2):
                    b0 = tab[ROW_BLOCK + r0 + 4 * i + 2 * k]
                    b1 = tab[ROW_BLOCK + r0 + 4 * i + 2 * k + 1]
                    hi = square(ah, b0, b1, t0, t1)
                    lo = square(al, b0, b1, t0, t1)
                    terms.append(
                        jnp.dot(
                            lhs[2 * i + k],
                            jnp.concatenate([hi, lo, hi], axis=0),
                            preferred_element_type=jnp.float32,
                        )
                    )
                acc[...] += terms[0] + terms[1]
                return inner

            lax.fori_loop(0, quads, rows_of, 0)
            for z in range(chunks):
                u_ref[z, s] = -acc[z * rows : (z + 1) * rows, :BLK]

            @pl.when(s + 1 < n1)
            def _():
                for z in range(chunks):
                    u_ref[z, s + 1] = -acc[z * rows : (z + 1) * rows, BLK:]

            return carry

        lax.fori_loop(0, (n1 - n0 + 1) // 2, columns, 0)
        return outer

    if fast:
        for j in range(sib):
            sibling(j, 0)
    else:
        lax.fori_loop(0, sib, sibling, 0)

    def clear(s, carry):
        u_ref[:, s] = jnp.zeros((chunks, rows, BLK), jnp.float32)
        return carry

    lax.fori_loop(tab[COL_START + sib], cap, clear, 0)


def unpack_kernel(tab, x_ref, o_ref):
    sib, _, cells = o_ref.shape
    blocks = cells // BLK

    def sibling(j, carry):
        for b in range(blocks):
            slot = tab[COL_SLOT + j * blocks + b]
            o_ref[j, :, b * BLK : (b + 1) * BLK] = jnp.where(
                slot >= 0, x_ref[jnp.maximum(slot, 0)], 0.0
            )
        return carry

    lax.fori_loop(0, sib, sibling, 0)


def inner_kernel(sib, tab, x_ref, hi_ref, lo_ref, o_ref):
    def sibling(j, carry):
        r0 = tab[ROW_START + j]
        r1 = tab[ROW_START + j + 1]

        def one(i, total):
            q = r0 + 2 * i
            after = jnp.where(q + 1 < r1, q + 1, q)
            x = jnp.concatenate([x_ref[q], jnp.where(after > q, x_ref[after], 0.0)], axis=1)
            x_hi = x.astype(jnp.bfloat16)
            x_lo = (x - x_hi.astype(jnp.float32)).astype(jnp.bfloat16)
            hi = jnp.concatenate([hi_ref[q], hi_ref[after]], axis=0)
            lo = jnp.concatenate([lo_ref[q], lo_ref[after]], axis=0)
            return total + jnp.dot(
                jnp.concatenate([x_hi, x_lo, x_hi], axis=1),
                jnp.concatenate([hi, hi, lo], axis=0),
                preferred_element_type=jnp.float32,
            )

        o_ref[j] = lax.fori_loop(
            0,
            (r1 - r0 + 1) // 2,
            one,
            jnp.zeros(o_ref.shape[1:], jnp.float32),
        )
        return carry

    lax.fori_loop(0, sib, sibling, 0)


def slots_kernel(sib, tab, x_ref, o_ref):
    blocks = o_ref.shape[2] // BLK

    def clear(d, carry):
        o_ref[d] = jnp.zeros(o_ref.shape[1:], jnp.float32)
        return carry

    lax.fori_loop(0, o_ref.shape[0], clear, 0)

    def sibling(j, carry):
        at = tab[OWNER + j]
        for b in range(blocks):
            slot = tab[ROW_SLOT + j * blocks + b]
            o_ref[at, :, b * BLK : (b + 1) * BLK] = jnp.where(
                slot >= 0, x_ref[jnp.maximum(slot, 0)], 0.0
            )
        return carry

    lax.fori_loop(0, sib, sibling, 0)


def place_kernel(tab, x_ref, o_ref):
    sib = x_ref.shape[0]

    def clear(d, carry):
        o_ref[d] = jnp.zeros(o_ref.shape[1:], jnp.float32)
        return carry

    lax.fori_loop(0, o_ref.shape[0], clear, 0)
    for j in range(sib):
        o_ref[tab[OWNER + j]] = x_ref[j]


def source_columns(tab, n_row):
    return [lax.rem(2 * n_row - r - tab[AT_ROW], n_row) for r in range(n_row)]


def lower_kernel(tab, x_ref, lower_ref):
    places = source_columns(tab, x_ref.shape[0])
    for b in range(lower_ref.shape[0] // BLK):
        stack = jnp.concatenate([x_ref[p, :, b * BLK : (b + 1) * BLK] for p in places], axis=0)
        lower_ref[b * BLK : (b + 1) * BLK, :] = stack.T


def diag_kernel(tab, x_ref, diag_ref, out_ref):
    total = jnp.concatenate([x_ref[p] for p in source_columns(tab, x_ref.shape[0])], axis=0)
    out_ref[...] = jnp.where(tab[PRESENT] > 0, diag_ref[...] - total, 0.0)


def ring_term(u, z, first, last, lead):
    part = lax.dynamic_index_in_dim(u, (z + 2 * u.shape[0]) % u.shape[0], 0, keepdims=False)
    part = part[first:last]
    return part if lead == 1 else part.reshape(lead, -1, *part.shape[1:])


def halves(parts, half, rows):
    return jnp.concatenate([lax.dynamic_slice_in_dim(x, half * rows, rows, 1) for x in parts])


def listed_products(cap, sib, table, scattered, a_hi, a_lo):
    row_cells, col_cells = a_hi.shape
    pieces, blocks, sub, width = scattered.shape
    near_chunks = lax.axis_size("row_0")
    half_rows = width // (near_chunks * lax.axis_size("row_1"))
    own = pl.pallas_call(
        functools.partial(pick_kernel, cap),
        out_shape=jax.ShapeDtypeStruct((cap, sub, width), jnp.float32),
        in_specs=[SMEM, VMEM],
        out_specs=VMEM,
        compiler_params=pltpu.CompilerParams(vmem_limit_bytes=8 << 20),
    )(table, scattered.reshape(pieces * blocks, sub, width))
    if cap < sib * blocks:
        right = turned(own, "col_x", 1)
        left = turned(own, "col_x", -1)
        beside = swapped(own, "col_y", 1)
        right_beside = turned(beside, "col_x", 1)
        left_beside = turned(beside, "col_x", -1)
        right_two = turned(right, "col_x", 1)
        left_two = turned(left_beside, "col_x", -1)
        g0 = jnp.stack([own, beside, right, left])
        g1 = jnp.stack([right_beside, left_beside, right_two, left_two])
        c0 = swapped(g0, "core", 1)
        c1 = swapped(g1, "core", 1)
    else:
        all_pieces = lax.all_to_all(
            jnp.broadcast_to(own[None], (pieces, *own.shape)), COL, 0, 0, tiled=True
        )
        g0, g1, c0, c1 = (all_pieces[i : i + 4] for i in range(0, pieces, 4))
    chunk = width // near_chunks
    u, p_hi, p_lo = pl.pallas_call(
        functools.partial(product_kernel, cap, sib),
        out_shape=(
            jax.ShapeDtypeStruct((near_chunks, cap, chunk, BLK), jnp.float32),
            jax.ShapeDtypeStruct((cap, BLK, width), jnp.bfloat16),
            jax.ShapeDtypeStruct((cap, BLK, width), jnp.bfloat16),
        ),
        in_specs=[SMEM] + [VMEM] * 6,
        out_specs=(VMEM, VMEM, VMEM),
        scratch_shapes=[
            pltpu.VMEM((cap, BLK, width), jnp.float32),
            pltpu.VMEM((row_cells // BLK // 2 + 1, width, 6 * BLK), jnp.bfloat16),
            pltpu.VMEM((width, 2 * BLK), jnp.float32),
        ],
        compiler_params=pltpu.CompilerParams(vmem_limit_bytes=(26 if cap < sib * blocks else 34) << 20),
    )(table, g0, g1, c0, c1, a_hi, a_lo)
    z = lax.axis_index("row_0")
    if cap < sib * blocks:
        strands = [(0, cap // 2, 1, 1), (cap // 2, cap, 3, -1)]
        near = [ring_term(u, z - way, first, last, lead) for first, last, lead, way in strands]
        for step in range(1, near_chunks):
            near = [
                turned(x, "row_0", way) + ring_term(u, z - way * (1 + step), first, last, lead)
                for x, (first, last, lead, way) in zip(near, strands)
            ]
        near = [x.reshape(-1, *x.shape[-2:]) for x in near]
    else:
        near = [jnp.sum(lax.all_to_all(u, "row_0", 0, 0, tiled=True), axis=0)]
    half = lax.axis_index("row_1")
    sent = halves(near, 1 - half, half_rows)
    kept = halves(near, half, half_rows)
    n_row = lax.axis_size(ROW)
    n_col = lax.axis_size(COL)
    spots = [(r, c) for r in range(n_row) for c in range(n_col)]
    across = [(r * n_col + c, r * n_col + (-r - c) % n_col) for r, c in spots]
    over = [(r * n_col + c, (r ^ 1) * n_col + (-(r ^ 1) - c) % n_col) for r, c in spots]
    along = [(r * n_col + k, (-r - k) % n_row * n_col + k) for r, k in spots]
    midway = lax.ppermute(kept, ROW + COL, across) + lax.ppermute(sent, ROW + COL, over)
    moved = lax.ppermute(midway, ROW + COL, along)
    sent, moved = lax.optimization_barrier((sent, moved))
    total = kept + swapped(sent, "row_1", 1)
    upper_part = pl.pallas_call(
        unpack_kernel,
        out_shape=jax.ShapeDtypeStruct((sib, half_rows, col_cells), jnp.float32),
        in_specs=[SMEM, VMEM],
        out_specs=VMEM,
        compiler_params=pltpu.CompilerParams(vmem_limit_bytes=8 << 20),
        cost_estimate=pl.CostEstimate(flops=0, transcendentals=0, bytes_accessed=1 << 20),
    )(table, total)
    slots = pl.pallas_call(
        functools.partial(slots_kernel, sib),
        out_shape=jax.ShapeDtypeStruct((n_col, half_rows, row_cells), jnp.float32),
        in_specs=[SMEM, VMEM],
        out_specs=VMEM,
        compiler_params=pltpu.CompilerParams(vmem_limit_bytes=8 << 20),
        cost_estimate=pl.CostEstimate(flops=0, transcendentals=0, bytes_accessed=2 << 20),
    )(table, moved)
    inner = pl.pallas_call(
        functools.partial(inner_kernel, sib),
        out_shape=jax.ShapeDtypeStruct((sib, half_rows, width), jnp.float32),
        in_specs=[SMEM] + [VMEM] * 3,
        out_specs=VMEM,
        compiler_params=pltpu.CompilerParams(vmem_limit_bytes=12 << 20),
        cost_estimate=pl.CostEstimate(
            flops=6 * cap * half_rows * BLK * width, transcendentals=0, bytes_accessed=6 << 20
        ),
    )(table, moved, p_hi, p_lo)
    return upper_part, slots, inner


def piece_columns():
    y = lax.axis_index("col_y")
    x = lax.axis_index("col_x")
    core = lax.axis_index("core")
    n_x = lax.axis_size("col_x")
    places = [(y, x), (1 - y, x), (y, x - 1), (y, x + 1)]
    places += [(1 - y, x - 1), (1 - y, x + 1), (y, x - 2), (1 - y, x + 2)]
    return jnp.stack(
        [
            (py * n_x + (px + n_x) % n_x) * 2 + pc
            for pc in (core, 1 - core)
            for py, px in places
        ]
    ).astype(jnp.int32)


def per_device(anc_inverse, l_store, diag_inv, block_lists, block_counts, sibling_columns):
    row_cells, col_cells = anc_inverse.shape
    width = l_store.shape[2]
    sib = sibling_columns.shape[0]
    n_col = lax.axis_size(COL)
    n_row = lax.axis_size(ROW)
    row_index = lax.axis_index(ROW)
    col_index = lax.axis_index(COL)
    blocks = row_cells // BLK
    cut = l_store[0].reshape(blocks, n_col, SUB, width).transpose(1, 0, 2, 3)
    scattered = lax.all_to_all(cut, COL, 0, 0, tiled=True)
    rounded = lax.reduce_precision(anc_inverse, 8, 7)
    a_hi = rounded.astype(jnp.bfloat16)
    a_lo = (anc_inverse - rounded).astype(jnp.bfloat16)

    listed = member_blocks(block_lists, block_counts, n_row * blocks)
    groups = listed.reshape(sib, n_row, blocks)
    most = jnp.max(jnp.sum(groups, axis=(0, 2)))
    row_code, row_start, row_slot = slot_tables(
        lax.dynamic_index_in_dim(groups, row_index, 1, keepdims=False)
    )
    col_code, col_start, col_slot = slot_tables(
        lax.dynamic_index_in_dim(groups, col_index, 1, keepdims=False)
    )
    owner = jnp.sum(
        jnp.where(
            (row_code // blocks)[:, None] == jnp.arange(sib, dtype=jnp.int32)[None, :],
            sibling_columns[None, :],
            0,
        ),
        axis=1,
    )
    table = jnp.concatenate(
        [
            padded(row_code % blocks, 64),
            padded(row_start, 8),
            padded(col_code % blocks, 64),
            padded(col_start, 8),
            padded(piece_columns(), 16),
            padded(row_slot, 64),
            padded(col_slot, 64),
            padded(owner * blocks + row_code % blocks, 64),
            padded(sibling_columns, 8),
            jnp.stack([jnp.any(sibling_columns == col_index).astype(jnp.int32), row_index]),
        ]
    )
    caps = [c for c in CAPS if c < sib * blocks] + [sib * blocks]
    which = sum((most > c).astype(jnp.int32) for c in caps[:-1])
    upper_part, slots, inner = lax.switch(
        which,
        [functools.partial(listed_products, c, sib) for c in caps],
        table,
        scattered,
        a_hi,
        a_lo,
    )
    place = lambda x: pl.pallas_call(
        place_kernel,
        out_shape=jax.ShapeDtypeStruct((n_col, *x.shape[1:]), jnp.float32),
        in_specs=[SMEM, VMEM],
        out_specs=VMEM,
        compiler_params=pltpu.CompilerParams(vmem_limit_bytes=8 << 20),
    )(table, x)
    gathered = lax.all_to_all(slots, COL, 0, 0, tiled=True)
    for bit in (1, 4):
        others = []
        for away in (bit, 2 * bit, 3 * bit):
            pairs = [
                (r * n_col + k, (r ^ away) * n_col + (k + r - (r ^ away)) % n_col)
                for r in range(n_row)
                for k in range(n_col)
            ]
            others.append(lax.ppermute(inner, ROW + COL, pairs))
        inner = (inner + others[0]) + (others[1] + others[2])
    gathered, inner = lax.optimization_barrier((gathered, inner))
    parts = lax.all_to_all(place(inner), COL, 0, 0, tiled=True)
    lower = pl.pallas_call(
        lower_kernel,
        out_shape=jax.ShapeDtypeStruct((row_cells, width), jnp.float32),
        in_specs=[SMEM, VMEM],
        out_specs=VMEM,
        compiler_params=pltpu.CompilerParams(vmem_limit_bytes=8 << 20),
        cost_estimate=pl.CostEstimate(flops=0, transcendentals=0, bytes_accessed=3 << 20),
    )(table, gathered)
    diag = pl.pallas_call(
        diag_kernel,
        out_shape=jax.ShapeDtypeStruct((width, width), jnp.float32),
        in_specs=[SMEM, VMEM, VMEM],
        out_specs=VMEM,
        compiler_params=pltpu.CompilerParams(vmem_limit_bytes=4 << 20),
    )(table, parts, diag_inv[0])
    return (upper_part, lower[None], diag[None])


def solution(mesh):
    finer = Mesh(mesh.devices.reshape(8, 2, 2, 4, 2), ROW + COL)
    return jax.shard_map(
        per_device,
        mesh=finer,
        in_specs=(P(ROW, COL), P(COL, ROW, None), P(COL, None, None), P(), P(), P()),
        out_specs=(P(None, ROW, COL), P(COL, ROW, None), P(COL, None, None)),
        check_vma=False,
    )
```
